128 devices in a mesh: plane: 2 (over x_hi), slab: 64 (over x_lo, y, z, core).
Axes of the slice: x: 4 (x_hi: 2, x_lo: 2; x = x_hi * 2 + x_lo), y: 4, z: 4, core: 2. Of those that a mesh axis runs over, the one named last changes fastest.
Arguments:
- kappa: float32 [2, 4096, 4096], P('plane', 'slab'), may hold values from -2.5 to 2.5
- ray_offsets: float32 [2, 64, 2, 8, 4096], P(None, 'slab', 'plane'), may hold values from -0.5 to 0.5
Outputs:
- deflection: float32 [2, 64, 2, 8, 4096], P(None, 'slab', 'plane')
- jacobian: float32 [4, 64, 2, 8, 4096], P(None, 'slab', 'plane')
The draws below stay inside these ranges and needn't reach their ends.
All inputs are finite; a program needn't handle non-finite values.
Results may differ from the reference program's by a relative error of at most 0.0003.
Values sent between devices are 32-bit elements; how exact they have to be, the bound alone decides.
No kernel may reach another device: no remote copies, remote signals or barrier semaphores. Data moves between devices by JAX's collectives and lax.ppermute only.
A program may use at most 64 MiB of HBM per device.

```python
import jax
import jax.numpy as jnp
from jax import lax

N = 4096
PLANES = 2
SLABS = 64
STEP = 4
RAYROWS = 8
MARGIN = 8
PATCH_ROWS = 16
BLOCK = 64


def draw_kappa(key, part):
    shape = (PLANES, N, N)
    return jnp.clip(0.5 * jax.random.normal(key, shape, jnp.float32), -2.5, 2.5)


def block_scale(key, extent, cuts, least, largest):
    loudness = 1.0
    for dim, parts in cuts:
        heights = jax.random.uniform(jax.random.fold_in(jax.random.fold_in(key, 6), dim), (parts,), jnp.float32, least / len(cuts), largest / len(cuts))
        loudness = loudness * jnp.repeat(jnp.exp(heights), extent[dim] // parts).reshape((-1,) + (1,) * (len(extent) - 1 - dim))
    return loudness


def setup_inputs(seed: int = 0) -> dict:
    arg_keys = jax.random.split(jax.random.key(seed), 3)
    return {
        "kappa": draw_kappa(jax.random.fold_in(arg_keys[2], 71), 0),
        "ray_offsets": jnp.clip(jax.random.uniform(arg_keys[1], (2, SLABS, PLANES, RAYROWS, N), jnp.float32, -0.5, 0.5) * block_scale(arg_keys[1], (2, SLABS, PLANES, RAYROWS, N), ((1, 64), (2, 2)), -0.4, 0.0), -0.5, 0.5),
    }


lens_ratio = 0.5
screen_modes = 4.0


def solve_plane(plane):
    length = plane.shape[0]
    indices = jnp.arange(length)
    folded = jnp.minimum(indices, length - indices).astype(plane.dtype)
    wave = (2.0 * jnp.pi / length) * folded
    screen = (2.0 * jnp.pi * screen_modes / length) ** 2
    denom = wave[:, None] ** 2 + wave[None, :] ** 2 + screen
    anchor = (indices[:, None] == 0) & (indices[None, :] == 0)
    factor = jnp.where(anchor, 0.0, -2.0 / denom).astype(plane.dtype)
    return jnp.real(jnp.fft.ifft2(jnp.fft.fft2(plane) * factor)).astype(plane.dtype)


def spline_terms(offset):
    magnitude = jnp.abs(offset)
    inside = magnitude < 1.0
    remain = jnp.maximum(2.0 - magnitude, 0.0)
    weights = jnp.where(inside, 2.0 / 3.0 - magnitude * magnitude + 0.5 * magnitude * magnitude * magnitude, remain * remain * remain / 6.0)
    slopes = jnp.sign(offset) * jnp.where(inside, -2.0 * magnitude + 1.5 * magnitude * magnitude, -0.5 * remain * remain)
    curves = jnp.where(inside, 3.0 * magnitude - 2.0, remain)
    return weights, slopes, curves


def lens_fields(plane_blocks, ycoord, xcoord):
    column_ids = jnp.arange(plane_blocks.shape[2]).astype(xcoord.dtype)
    row_ids = jnp.arange(plane_blocks.shape[0]).astype(ycoord.dtype)
    x_weights = jnp.stack(spline_terms(xcoord[:, :, None] - column_ids), axis=1)
    across = jnp.einsum("pbc,bkrc->bkpr", plane_blocks, x_weights, precision=lax.Precision.HIGHEST)
    down_weights, down_slopes, down_curves = spline_terms(ycoord[:, None, :] - row_ids[:, None])
    slope_down = jnp.sum(down_slopes * across[:, 0], axis=1)
    slope_across = jnp.sum(down_weights * across[:, 1], axis=1)
    bend_down = jnp.sum(down_curves * across[:, 0], axis=1)
    bend_across = jnp.sum(down_weights * across[:, 2], axis=1)
    bend_mixed = jnp.sum(down_slopes * across[:, 1], axis=1)
    return slope_down, slope_across, bend_down, bend_across, bend_mixed


def ray_row_outputs(window, shift_y, shift_x):
    grid_width = shift_y.shape[0]
    block_count = grid_width // BLOCK
    column_view = window.reshape(window.shape[0], PATCH_ROWS, block_count + 1, BLOCK)
    blocks = jnp.concatenate([column_view[:, :, :-1], column_view[:, :, 1:]], axis=3)
    centre_row = PATCH_ROWS // 2 - 1
    ycoord = centre_row + STEP * shift_y.reshape(block_count, BLOCK)
    xcoord = BLOCK // 2 + jnp.arange(BLOCK).astype(shift_x.dtype) + shift_x.reshape(block_count, BLOCK)
    first = lens_fields(blocks[0], ycoord, xcoord)
    second = lens_fields(blocks[1], ycoord - lens_ratio * first[0], xcoord - lens_ratio * first[1])
    hess_yy, hess_xx, hess_xy = first[2], first[3], first[4]
    other_yy, other_xx, other_xy = second[2], second[3], second[4]
    lensed_yy = 1.0 - lens_ratio * hess_yy
    lensed_xx = 1.0 - lens_ratio * hess_xx
    lensed_xy = -lens_ratio * hess_xy
    entry_yy = 1.0 - hess_yy - (other_yy * lensed_yy + other_xy * lensed_xy)
    entry_yx = -hess_xy - (other_yy * lensed_xy + other_xy * lensed_xx)
    entry_xy = -hess_xy - (other_xy * lensed_yy + other_xx * lensed_xy)
    entry_xx = 1.0 - hess_xx - (other_xy * lensed_xy + other_xx * lensed_xx)
    deflect = jnp.stack([first[0] + second[0], first[1] + second[1]]).reshape(2, grid_width)
    jacob = jnp.stack([entry_yy, entry_yx, entry_xy, entry_xx]).reshape(4, grid_width)
    return deflect, jacob


def reference(kappa, ray_offsets):
    potentials = jnp.stack([solve_plane(kappa[0]), solve_plane(kappa[1])])
    padded = jnp.pad(potentials, ((0, 0), (MARGIN, MARGIN), (BLOCK // 2, BLOCK // 2)), mode="wrap")
    ray_total = SLABS * PLANES * RAYROWS
    offsets = ray_offsets.reshape(2, ray_total, N)
    centre_row = PATCH_ROWS // 2 - 1

    def one_row(packed):
        ray_row, shift_y, shift_x = packed
        first_row = (STEP * ray_row + (STEP // 2 - centre_row + MARGIN)).astype(jnp.int32)
        window = lax.dynamic_slice_in_dim(padded, first_row, PATCH_ROWS, 1)
        return ray_row_outputs(window, shift_y, shift_x)

    deflect, jacob = lax.map(one_row, (jnp.arange(ray_total, dtype=jnp.int32), offsets[0], offsets[1]))
    deflection = jnp.transpose(deflect, (1, 0, 2)).reshape(2, SLABS, PLANES, RAYROWS, N)
    jacobian = jnp.transpose(jacob, (1, 0, 2)).reshape(4, SLABS, PLANES, RAYROWS, N)
    return deflection, jacobian
```

```python
import functools
import math

import jax
import jax.numpy as jnp
import numpy as np
from jax import lax
from jax.experimental import pallas as pl
from jax.experimental.pallas import tpu as pltpu
from jax.sharding import PartitionSpec as P

N = 4096
OUTER = 32
SLABS = 64
WIN = 48
LEAD = 5
HIGHEST = lax.Precision.HIGHEST
lens_ratio = 0.5
screen_modes = 4.0


def angles(left, right, length):
    return (np.outer(left, right) % length) * (2.0 * np.pi / length)


def cas_pair(left, right, length):
    a = angles(left, right, length)
    return np.cos(a) + np.sin(a), np.cos(a) - np.sin(a)


def f32(table):
    return np.asarray(table, np.float32)


@functools.cache
def tables():
    out = {}
    lane = np.arange(128)
    plus, minus = cas_pair(lane, lane, 128)
    out["row_fwd"] = f32(np.concatenate([plus.T, minus.T], axis=1))
    turn = angles(np.arange(OUTER), lane, N)
    out["row_turn"] = f32(np.stack([np.cos(turn), np.sin(turn)]))
    out["row_inv"] = f32(0.5 * np.concatenate([plus, -minus], axis=1))
    sixty = np.arange(64)
    plus, minus = cas_pair(sixty, sixty, 64)
    two = np.eye(2)
    out["col_fwd"] = f32(np.concatenate([np.kron(two, plus), np.kron(two, minus)], axis=0))
    turn = angles(sixty, np.concatenate([sixty, sixty]), N)
    out["col_turn"] = f32(np.stack([np.cos(turn), np.sin(turn)]))
    inv, turns = [], []
    for p in range(2):
        rows = 32 * p - LEAD + np.arange(WIN)
        plus, minus = cas_pair(sixty, rows, 64)
        pad = np.zeros((128, 32))
        inv.append(np.concatenate([np.kron(two, plus), pad, -np.kron(two, minus), pad], axis=1))
        turn = angles(sixty, np.concatenate([rows, rows, np.zeros(32, rows.dtype)]), N)
        turns.append(np.stack([np.cos(turn), np.sin(turn)]))
    out["col_inv"] = f32(0.5 * np.stack(inv))
    out["col_back"] = f32(np.stack(turns))
    ids = np.arange(64)[:, None] + 64 * np.concatenate([sixty, sixty])[None, :]
    wave = 2.0 * np.pi / N * np.minimum(ids, N - ids)
    out["wave2"] = f32(wave**2)
    return out


def cmul(re, im, c, s):
    if abs(s) < 1e-12 and abs(c - 1.0) < 1e-12:
        return re, im
    if abs(c) < 1e-12 and abs(s - 1.0) < 1e-12:
        return (None if im is None else -im), re
    if im is None:
        return re * c, re * s
    if re is None:
        return im * (-s), im * c
    if abs(c - s) < 1e-12:
        return (re - im) * c, (re + im) * c
    if abs(c + s) < 1e-12:
        return (re + im) * c, (im - re) * c
    return re * c - im * s, re * s + im * c


def add(a, b):
    return b if a is None else a if b is None else a + b


def sub(a, b):
    return a if b is None else -b if a is None else a - b


def neg(a):
    return None if a is None else -a


def real_to_half(xs):
    n = len(xs)
    if n == 2:
        return [(xs[0] + xs[1], None), (xs[0] - xs[1], None)]
    even, odd = real_to_half(xs[0::2]), real_to_half(xs[1::2])
    half = n // 2
    out = [None] * (half + 1)
    for k in range(half // 2 + 1):
        c, s = math.cos(2 * math.pi * k / n), math.sin(2 * math.pi * k / n)
        tr, ti = cmul(*odd[k], c, s)
        er, ei = even[k]
        out[k] = (add(er, tr), add(ei, ti))
        if half - k != k:
            out[half - k] = (sub(er, tr), sub(ti, ei))
    return out


def half_to_real(xs):
    half = len(xs) - 1
    n = 2 * half
    if n == 2:
        return [xs[0][0] + xs[1][0], xs[0][0] - xs[1][0]]
    even, odd = [], []
    for k in range(half // 2 + 1):
        ar, ai = xs[k]
        br, bi = xs[half - k]
        if k == half - k:
            even.append((ar + ar, None))
            odd.append((-(ai + ai), None))
            continue
        even.append((add(ar, br), sub(ai, bi)))
        c, s = math.cos(2 * math.pi * k / n), math.sin(2 * math.pi * k / n)
        odd.append(cmul(sub(ar, br), add(ai, bi), c, s))
    evens, odds = half_to_real(even), half_to_real(odd)
    return [v for pair in zip(evens, odds) for v in pair]


def row8(ref, *index):
    return jnp.broadcast_to(ref[index], (8, 128))


def turned(re, im, c, s):
    if im is None:
        return re * c, re * s
    return re * c - im * s, re * s + im * c


def forward_outer(xs, turn_ref, store):
    n = len(xs)
    half = real_to_half(xs)
    for m in range(n):
        re, im = half[m] if m <= n // 2 else (half[n - m][0], neg(half[n - m][1]))
        store(m, *turned(re, im, row8(turn_ref, 0, slice(m, m + 1)), row8(turn_ref, 1, slice(m, m + 1))))


def inverse_outer(load, n, turn_ref, *lead):
    def value(m):
        re, im = load(m)
        return turned(re, im, row8(turn_ref, *lead, 0, slice(m, m + 1)), row8(turn_ref, *lead, 1, slice(m, m + 1)))

    spectrum = []
    for m in range(n // 2 + 1):
        re, im = value(m)
        if m in (0, n // 2):
            spectrum.append((re + re, None))
        else:
            ro, io = value(n - m)
            spectrum.append((re + ro, im - io))
    return half_to_real(spectrum)


def rows_kernel(kappa_ref, weight_ref, turn_ref, out_ref, mid):
    def group(g, carry):
        rows = pl.ds(pl.multiple_of(8 * g, 8), 8)
        xs = [kappa_ref[rows, 128 * j : 128 * j + 128] for j in range(OUTER)]

        def store(m, re, im):
            spot = pl.ds(pl.multiple_of(64 * m + 8 * g, 8), 8)
            mid[spot, 0:128] = re
            mid[spot, 128:256] = im

        forward_outer(xs, turn_ref, store)
        return carry

    lax.fori_loop(0, 8, group, 0)

    def pair(i, carry):
        spot = pl.ds(pl.multiple_of(128 * i, 128), 128)
        out_ref[spot, :] = lax.dot_general(
            weight_ref[...], mid[spot, :], (((1,), (1,)), ((), ())),
            precision=HIGHEST, preferred_element_type=jnp.float32,
        )
        return carry

    lax.fori_loop(0, 16, pair, 0)


def columns_kernel(in_ref, fwd_ref, turn_ref, wave_ref, inv_ref, back_ref, out_ref, mid, spec, strips):
    owner = lax.axis_index("slab")
    base = 2 * lax.div(owner, 4) + 1024 * lax.rem(owner, 4)
    lane = lax.broadcasted_iota(jnp.int32, (8, 128), 1)
    sub8 = lax.broadcasted_iota(jnp.int32, (8, 128), 0)
    screen = (2.0 * math.pi * screen_modes / N) ** 2

    def group(g, carry):
        rows = pl.ds(pl.multiple_of(8 * g, 8), 8)
        xs = [in_ref[s, rows, :] for s in range(SLABS)]

        def store(m, re, im):
            mid[8 * m : 8 * m + 8, 0:128] = re
            mid[8 * m : 8 * m + 8, 128:256] = im

        forward_outer(xs, turn_ref, store)
        spec[...] = jnp.dot(mid[...], fwd_ref[...], precision=HIGHEST, preferred_element_type=jnp.float32)
        ids = base + jnp.where(lane >= 64, 1, 0) + 32 * (8 * g + sub8)
        wave = (2.0 * math.pi / N) * jnp.minimum(ids, N - ids).astype(jnp.float32)
        mine = wave * wave + screen
        for m in range(SLABS):
            factor = -2.0 / ((mine + row8(wave_ref, slice(m, m + 1))) * float(N * N))
            if m == 0:
                factor = jnp.where((ids == 0) & (lane == 0), 0.0, factor)
            spec[8 * m : 8 * m + 8, :] = spec[8 * m : 8 * m + 8, :] * factor
        for p in range(2):
            mid[...] = jnp.dot(spec[...], inv_ref[p], precision=HIGHEST, preferred_element_type=jnp.float32)
            values = inverse_outer(
                lambda m: (mid[8 * m : 8 * m + 8, 0:128], mid[8 * m : 8 * m + 8, 128:256]), SLABS, back_ref, p
            )
            for s in range(SLABS):
                strips[p * SLABS + s, rows, :] = values[s]
        return carry

    lax.fori_loop(0, 4, group, 0)

    def pack(d, carry):
        last = strips[d, 24:32, :]
        for k in range(3):
            moved = last if k == 3 else pltpu.roll(last, (96 - 32 * k) % 128, 1)
            out_ref[d, 8 * k : 8 * k + 8, :] = jnp.where(lane < 96, strips[d, 8 * k : 8 * k + 8, :], moved)
        return carry

    lax.fori_loop(0, 2 * SLABS, pack, 0, unroll=4)


def spline_weights(f):
    e = 1.0 - f
    f2, e2 = f * f, e * e
    f3, e3 = f2 * f, e2 * e
    sixth, third = 1.0 / 6.0, 2.0 / 3.0
    value = [e3 * sixth, third - f2 + 0.5 * f3, third - e2 + 0.5 * e3, f3 * sixth]
    slope = [-0.5 * e2, 1.5 * f2 - 2.0 * f, 2.0 * e - 1.5 * e2, 0.5 * f2]
    curve = [e, 3.0 * f - 2.0, 1.0 - 3.0 * f, f]
    return value, slope, curve


def dot4(ws, vs):
    return (ws[0] * vs[0] + ws[1] * vs[1]) + (ws[2] * vs[2] + ws[3] * vs[3])


def stencil(taps, xw, yw):
    flat = [dot4(xw[0], row) for row in taps]
    slope = [dot4(xw[1], row) for row in taps]
    curve = [dot4(xw[2], row) for row in taps]
    return dot4(yw[1], flat), dot4(yw[0], slope), dot4(yw[2], flat), dot4(yw[0], curve), dot4(yw[1], slope)


def rays_kernel(in_ref, inv_ref, turn_ref, off_ref, deflect_ref, jacob_ref, mid, near, even, odd):
    lane = lax.broadcasted_iota(jnp.int32, (8, 128), 1)

    for q in range(2):
        def unpack(i, carry):
            parts = []
            for d in range(4):
                got = [in_ref[q * SLABS + 4 * i + d, 8 * k : 8 * k + 8, :] for k in range(3)]
                moved = [pltpu.roll(got[k], 32 + 32 * k, 1) for k in range(3)]
                parts += got
                parts.append(jnp.where(lane < 32, moved[0], jnp.where(lane < 64, moved[1], moved[2])))
            block = jnp.transpose(jnp.concatenate(parts, axis=0))[: 2 * WIN]
            spot = pl.ds(pl.multiple_of(2 * WIN * i, 8), 2 * WIN)
            mid[spot, :] = jnp.dot(block, inv_ref[...], precision=HIGHEST, preferred_element_type=jnp.float32)
            return carry

        lax.fori_loop(0, 16, unpack, 0)

        def finish(g, carry):
            def load(m):
                spot = pl.ds(pl.multiple_of(WIN * m + 8 * g, 8), 8)
                return mid[spot, 0:128], mid[spot, 128:256]

            values = inverse_outer(load, OUTER, turn_ref)

            def spot(t):
                return pl.ds(pl.multiple_of(WIN * t + 8 * g, 8), 8)

            if q == 0:
                for t in range(OUTER):
                    near[2, spot(t), :] = values[t]
                for d in (-2, -1, 1, 2):
                    moved = [pltpu.roll(v, (-d) % 128, 1) for v in values]
                    for t in range(OUTER):
                        if d < 0:
                            v = jnp.where(lane < -d, moved[t - 1], moved[t])
                        else:
                            v = jnp.where(lane < 128 - d, moved[t], moved[(t + 1) % OUTER])
                        near[2 + d, spot(t), :] = v
            else:
                moved = [pltpu.roll(v, 32, 1) for v in values]
                for t in range(OUTER):
                    even[spot(t), :] = jnp.where(lane < 32, moved[t - 1], moved[t])
                moved = [pltpu.roll(v, 96, 1) for v in values]
                for t in range(OUTER):
                    odd[spot(t), :] = jnp.where(lane < 96, moved[t], moved[(t + 1) % OUTER])
            return carry

        lax.fori_loop(0, WIN // 8, finish, 0)

    def tile(t, carry):
        cols = pl.ds(pl.multiple_of(128 * t, 128), 128)
        off_y = off_ref[0, :, cols]
        off_x = off_ref[1, :, cols]
        zero = jnp.zeros((8, 128), jnp.float32)
        rel_y = 4.0 * off_y
        low_y = jnp.floor(rel_y)
        left = off_x < 0.0
        frac_x = jnp.where(left, off_x + 1.0, off_x)
        hit = {v: low_y == float(v) for v in range(-2, 3)}
        taps = [[zero] * 4 for _ in range(4)]
        for j in range(4, 11):
            rows = [near[d, pl.ds(WIN * t + j, 8, stride=4), :] for d in range(5)]
            cells = [jnp.where(left, rows[c], rows[c + 1]) for c in range(4)]
            for r in range(4):
                if j - 6 - r in hit:
                    for c in range(4):
                        taps[r][c] = jnp.where(hit[j - 6 - r], cells[c], taps[r][c])
        first = stencil(taps, spline_weights(frac_x), spline_weights(rel_y - low_y))
        pos_y = (7.0 + rel_y) - lens_ratio * first[0]
        start = (32 + lax.rem(lane, 64)).astype(jnp.float32)
        pos_x = (start + off_x) - lens_ratio * first[1]
        low_y = jnp.floor(pos_y)
        low_x = jnp.floor(pos_x)
        xw = spline_weights(pos_x - low_x)
        yw = spline_weights(pos_y - low_y)
        cell_x = jnp.clip(low_x, -8.0, 136.0).astype(jnp.int32)
        cell_y = jnp.clip(low_y, -8.0, 32.0).astype(jnp.int32)
        spots = [cell_x + (c - 1) for c in range(4)]
        inside = [(s >= 0) & (s < 128) for s in spots]
        xw = [[jnp.where(inside[c], w[c], 0.0) for c in range(4)] for w in xw]
        spots = [jnp.clip(s, 0, 127) for s in spots]
        is_even = lane < 64
        hit = {v: cell_y == v for v in range(-2, 17)}
        taps = [[zero] * 4 for _ in range(4)]
        for j in range(16):
            ev = even[pl.ds(WIN * t + j, 8, stride=4), :]
            od = odd[pl.ds(WIN * t + j, 8, stride=4), :]
            for c in range(4):
                cell = jnp.where(
                    is_even,
                    jnp.take_along_axis(ev, spots[c], axis=1),
                    jnp.take_along_axis(od, spots[c], axis=1),
                )
                for r in range(4):
                    taps[r][c] = jnp.where(hit[j + 1 - r], cell, taps[r][c])
        second = stencil(taps, xw, yw)
        hess_yy, hess_xx, hess_xy = first[2], first[3], first[4]
        other_yy, other_xx, other_xy = second[2], second[3], second[4]
        lensed_yy = 1.0 - lens_ratio * hess_yy
        lensed_xx = 1.0 - lens_ratio * hess_xx
        lensed_xy = -lens_ratio * hess_xy
        deflect_ref[0, :, cols] = first[0] + second[0]
        deflect_ref[1, :, cols] = first[1] + second[1]
        jacob_ref[0, :, cols] = 1.0 - hess_yy - (other_yy * lensed_yy + other_xy * lensed_xy)
        jacob_ref[1, :, cols] = -hess_xy - (other_yy * lensed_xy + other_xy * lensed_xx)
        jacob_ref[2, :, cols] = -hess_xy - (other_xy * lensed_yy + other_xx * lensed_xy)
        jacob_ref[3, :, cols] = 1.0 - hess_xx - (other_xy * lensed_xy + other_xx * lensed_xx)
        return carry

    lax.fori_loop(0, OUTER, tile, 0)


def vmem(shape):
    return pltpu.VMEM(shape, jnp.float32)


def call(kernel, name, args, outs, scratch):
    return pl.pallas_call(
        kernel,
        name=name,
        out_shape=outs,
        in_specs=[pl.BlockSpec(memory_space=pltpu.VMEM)] * len(args),
        out_specs=jax.tree.map(lambda _: pl.BlockSpec(memory_space=pltpu.VMEM), outs),
        scratch_shapes=scratch,
        compiler_params=pltpu.CompilerParams(vmem_limit_bytes=60 * 1024 * 1024),
    )(*args)


def shape(*dims):
    return jax.ShapeDtypeStruct(dims, jnp.float32)


def on_device(kappa, ray_offsets):
    tab = tables()
    spectra = call(
        rows_kernel, "rows", (kappa[0], tab["row_fwd"], tab["row_turn"]), shape(2048, 128), [vmem((2048, 256))]
    )
    columns = lax.all_to_all(spectra.reshape(SLABS, 32, 128), "slab", split_axis=0, concat_axis=0, tiled=True)
    strips = call(
        columns_kernel,
        "columns",
        (columns, tab["col_fwd"], tab["col_turn"], tab["wave2"], tab["col_inv"], tab["col_back"]),
        shape(2 * SLABS, 24, 128),
        [vmem((512, 256)), vmem((512, 128)), vmem((2 * SLABS, 32, 128))],
    )
    windows = lax.all_to_all(strips, ("plane", "slab"), split_axis=0, concat_axis=0, tiled=True)
    deflection, jacobian = call(
        rays_kernel,
        "rays",
        (windows, tab["row_inv"], tab["row_turn"], ray_offsets[:, 0, 0]),
        (shape(2, 8, N), shape(4, 8, N)),
        [vmem((OUTER * WIN, 256)), vmem((5, OUTER * WIN, 128)), vmem((OUTER * WIN, 128)), vmem((OUTER * WIN, 128))],
    )
    return deflection[:, None, None], jacobian[:, None, None]


def solution(mesh):
    placed = (P("plane", "slab", None), P(None, "slab", "plane", None, None))
    return jax.shard_map(
        on_device,
        mesh=mesh,
        in_specs=placed,
        out_specs=(P(None, "slab", "plane", None, None), P(None, "slab", "plane", None, None)),
        check_vma=False,
    )
```

```python
import functools
import math

import jax
import jax.numpy as jnp
import numpy as np
from jax import lax
from jax.experimental import pallas as pl
from jax.experimental.pallas import tpu as pltpu
from jax.sharding import PartitionSpec as P

N = 4096
OUTER = 32
SLABS = 64
PATCH_ROWS = 16
WIN = 48
UNROLL = 1
LEAD = 5
lens_ratio = 0.5
screen_modes = 4.0


def angles(left, right, length):
    return (np.outer(left, right) % length) * (2.0 * np.pi / length)


def cas_pair(left, right, length):
    a = angles(left, right, length)
    return np.cos(a) + np.sin(a), np.cos(a) - np.sin(a)


def f32(table):
    return np.asarray(table, np.float32)


def parts(table, count):
    out = []
    for _ in range(count):
        out.append(np.asarray(table, jnp.bfloat16))
        table = table - np.asarray(out[-1], np.float64)
    return out


@functools.cache
def tables():
    out = {}
    lane = np.arange(128)
    plus, minus = cas_pair(lane, lane, 128)
    out["row_fwd"] = np.concatenate(parts(np.concatenate([plus.T, minus.T], axis=1), 2), axis=0)
    turn = angles(np.arange(OUTER), lane, N)
    out["row_turn"] = f32(np.stack([np.cos(turn), np.sin(turn)]))
    out["row_inv"] = np.stack(parts(0.5 * np.concatenate([plus, -minus], axis=1), 3))
    sixty = np.arange(64)
    plus, minus = cas_pair(sixty, sixty, 64)
    two = np.eye(2)
    both = np.concatenate([np.kron(two, plus), np.kron(two, minus)], axis=0)
    out["col_fwd"] = np.concatenate(parts(both, 2), axis=1)
    turn = angles(sixty, np.concatenate([sixty, sixty]), N)
    out["col_turn"] = f32(np.stack([np.cos(turn), np.sin(turn)]))
    inv, turns = [], []
    for p in range(2):
        rows = 32 * p - LEAD + np.arange(WIN)
        plus, minus = cas_pair(sixty, rows, 64)
        pad = np.zeros((128, 32))
        inv.append(np.concatenate([np.kron(two, plus), pad, -np.kron(two, minus), pad], axis=1))
        turn = angles(sixty, np.concatenate([rows, rows, np.zeros(32, rows.dtype)]), N)
        turns.append(np.stack([np.cos(turn), np.sin(turn)]))
    out["col_inv"] = np.stack([np.stack(parts(0.5 * table, 3)) for table in inv])
    out["col_back"] = f32(np.stack(turns))
    ids = np.arange(64)[:, None] + 64 * np.concatenate([sixty, sixty])[None, :]
    wave = 2.0 * np.pi / N * np.minimum(ids, N - ids)
    out["wave2"] = f32(wave**2)
    return out


def cmul(re, im, c, s):
    if abs(s) < 1e-12 and abs(c - 1.0) < 1e-12:
        return re, im
    if abs(c) < 1e-12 and abs(s - 1.0) < 1e-12:
        return (None if im is None else -im), re
    if im is None:
        return re * c, re * s
    if re is None:
        return im * (-s), im * c
    if abs(c - s) < 1e-12:
        return (re - im) * c, (re + im) * c
    if abs(c + s) < 1e-12:
        return (re + im) * c, (im - re) * c
    return re * c - im * s, re * s + im * c


def add(a, b):
    return b if a is None else a if b is None else a + b


def sub(a, b):
    return a if b is None else -b if a is None else a - b


def neg(a):
    return None if a is None else -a


def real_to_half(xs):
    n = len(xs)
    if n == 2:
        return [(xs[0] + xs[1], None), (xs[0] - xs[1], None)]
    even, odd = real_to_half(xs[0::2]), real_to_half(xs[1::2])
    half = n // 2
    out = [None] * (half + 1)
    for k in range(half // 2 + 1):
        c, s = math.cos(2 * math.pi * k / n), math.sin(2 * math.pi * k / n)
        tr, ti = cmul(*odd[k], c, s)
        er, ei = even[k]
        out[k] = (add(er, tr), add(ei, ti))
        if half - k != k:
            out[half - k] = (sub(er, tr), sub(ti, ei))
    return out


def half_to_real(xs):
    half = len(xs) - 1
    n = 2 * half
    if n == 2:
        return [xs[0][0] + xs[1][0], xs[0][0] - xs[1][0]]
    even, odd = [], []
    for k in range(half // 2 + 1):
        ar, ai = xs[k]
        br, bi = xs[half - k]
        if k == half - k:
            even.append((ar + ar, None))
            odd.append((-(ai + ai), None))
            continue
        even.append((add(ar, br), sub(ai, bi)))
        c, s = math.cos(2 * math.pi * k / n), math.sin(2 * math.pi * k / n)
        odd.append(cmul(sub(ar, br), add(ai, bi), c, s))
    evens, odds = half_to_real(even), half_to_real(odd)
    return [v for pair in zip(evens, odds) for v in pair]


def row8(ref, *index):
    return jnp.broadcast_to(ref[index], (8, 128))


def turned(re, im, c, s):
    if im is None:
        return re * c, re * s
    return re * c - im * s, re * s + im * c


def forward_outer(xs, turn_ref, store):
    n = len(xs)
    half = real_to_half(xs)
    for m in range(n):
        re, im = half[m] if m <= n // 2 else (half[n - m][0], neg(half[n - m][1]))
        store(m, *turned(re, im, row8(turn_ref, 0, slice(m, m + 1)), row8(turn_ref, 1, slice(m, m + 1))))


def inverse_outer(load, n, turn_ref, *lead):
    def value(m):
        re, im = load(m)
        return turned(re, im, row8(turn_ref, *lead, 0, slice(m, m + 1)), row8(turn_ref, *lead, 1, slice(m, m + 1)))

    spectrum = []
    for m in range(n // 2 + 1):
        re, im = value(m)
        if m in (0, n // 2):
            spectrum.append((re + re, None))
        else:
            ro, io = value(n - m)
            spectrum.append((re + ro, im - io))
    return half_to_real(spectrum)


def split(x, count):
    out = []
    for i in range(count):
        out.append(x.astype(jnp.bfloat16))
        if i + 1 < count:
            x = x - out[-1].astype(jnp.float32)
    return out


def fine_dot(x, w):
    a, b, c = split(x, 3)
    w0, w1, w2 = w[0], w[1], w[2]
    left = jnp.concatenate([a, b, a, b, a, c], axis=1)
    right = jnp.concatenate([w0, w0, w1, w1, w2, w0], axis=0)
    return jnp.dot(left, right, preferred_element_type=jnp.float32)


def rows_kernel(kappa_ref, weight_ref, turn_ref, out_ref, mid):
    def group(g, carry):
        rows = pl.ds(pl.multiple_of(8 * g, 8), 8)
        xs = [kappa_ref[rows, 128 * j : 128 * j + 128] for j in range(OUTER)]

        def store(m, re, im):
            spot = pl.ds(pl.multiple_of(64 * m + 8 * g, 8), 8)
            mid[spot, 0:128] = re
            mid[spot, 128:256] = im

        forward_outer(xs, turn_ref, store)
        return carry

    lax.fori_loop(0, 8, group, 0)

    def pair(i, carry):
        spot = pl.ds(pl.multiple_of(128 * i, 128), 128)
        left = jnp.concatenate([weight_ref[...]] * 2, axis=1)
        right = jnp.concatenate(split(mid[spot, :], 2), axis=1)
        both = lax.dot_general(left, right, (((1,), (1,)), ((), ())), preferred_element_type=jnp.float32)
        out_ref[spot, :] = both[:128] + both[128:]
        return carry

    lax.fori_loop(0, 16, pair, 0)


def columns_kernel(in_ref, fwd_ref, turn_ref, wave_ref, inv_ref, back_ref, out_ref, mid, spec, strips):
    owner = lax.axis_index("slab")
    base = 2 * lax.div(owner, 4) + 1024 * lax.rem(owner, 4)
    lane = lax.broadcasted_iota(jnp.int32, (8, 128), 1)
    sub8 = lax.broadcasted_iota(jnp.int32, (8, 128), 0)
    screen = (2.0 * math.pi * screen_modes / N) ** 2

    def group(g, carry):
        rows = pl.ds(pl.multiple_of(8 * g, 8), 8)
        xs = [in_ref[s, rows, :] for s in range(SLABS)]

        def store(m, re, im):
            mid[8 * m : 8 * m + 8, 0:128] = re
            mid[8 * m : 8 * m + 8, 128:256] = im

        forward_outer(xs, turn_ref, store)
        left = jnp.concatenate(split(mid[...], 2), axis=1)
        right = jnp.concatenate([fwd_ref[...]] * 2, axis=0)
        both = jnp.dot(left, right, preferred_element_type=jnp.float32)
        spec[...] = both[:, :128] + both[:, 128:]
        ids = base + jnp.where(lane >= 64, 1, 0) + 32 * (8 * g + sub8)
        wave = (2.0 * math.pi / N) * jnp.minimum(ids, N - ids).astype(jnp.float32)
        mine = wave * wave + screen
        for m in range(SLABS):
            factor = -2.0 / ((mine + row8(wave_ref, slice(m, m + 1))) * float(N * N))
            if m == 0:
                factor = jnp.where((ids == 0) & (lane == 0), 0.0, factor)
            spec[8 * m : 8 * m + 8, :] = spec[8 * m : 8 * m + 8, :] * factor
        for p in range(2):
            mid[...] = fine_dot(spec[...], inv_ref[p])
            values = inverse_outer(
                lambda m: (mid[8 * m : 8 * m + 8, 0:128], mid[8 * m : 8 * m + 8, 128:256]), SLABS, back_ref, p
            )
            for s in range(SLABS):
                strips[p * SLABS + s, rows, :] = values[s]
        return carry

    lax.fori_loop(0, 4, group, 0)

    def pack(d, carry):
        last = strips[d, 24:32, :]
        for k in range(3):
            moved = last if k == 3 else pltpu.roll(last, (96 - 32 * k) % 128, 1)
            out_ref[d, 8 * k : 8 * k + 8, :] = jnp.where(lane < 96, strips[d, 8 * k : 8 * k + 8, :], moved)
        return carry

    lax.fori_loop(0, 2 * SLABS, pack, 0, unroll=4)


def spline_weights(f):
    e = 1.0 - f
    f2, e2 = f * f, e * e
    f3, e3 = f2 * f, e2 * e
    sixth, third = 1.0 / 6.0, 2.0 / 3.0
    value = [e3 * sixth, third - f2 + 0.5 * f3, third - e2 + 0.5 * e3, f3 * sixth]
    slope = [-0.5 * e2, 1.5 * f2 - 2.0 * f, 2.0 * e - 1.5 * e2, 0.5 * f2]
    curve = [e, 3.0 * f - 2.0, 1.0 - 3.0 * f, f]
    return value, slope, curve


def dot4(ws, vs):
    return (ws[0] * vs[0] + ws[1] * vs[1]) + (ws[2] * vs[2] + ws[3] * vs[3])


def stencil(taps, xw, yw):
    rows = list(zip(*taps))
    flat = [dot4(xw[0], row) for row in rows]
    slope = [dot4(xw[1], row) for row in rows]
    curve = [dot4(xw[2], row) for row in rows]
    return dot4(yw[1], flat), dot4(yw[0], slope), dot4(yw[2], flat), dot4(yw[0], curve), dot4(yw[1], slope)


def kept(weights, first, count):
    inside = [(first + c >= 0) & (first + c < count) for c in range(4)]
    return [[jnp.where(inside[c], w[c], 0.0) for c in range(4)] for w in weights]


def lane_gather(values, spots):
    dims = lax.GatherDimensionNumbers(
        offset_dims=(), collapsed_slice_dims=(1,), start_index_map=(1,),
        operand_batching_dims=(0,), start_indices_batching_dims=(0,),
    )
    return lax.gather(
        values, spots[..., None], dims, (1, 1), mode=lax.GatherScatterMode.PROMISE_IN_BOUNDS
    )


def rays_kernel(in_ref, inv_ref, turn_ref, off_ref, deflect_ref, jacob_ref, mid, near, even, odd):
    lane = lax.broadcasted_iota(jnp.int32, (8, 128), 1)

    for q in range(2):
        def unpack(i, carry):
            parts = []
            for d in range(4):
                got = [in_ref[q * SLABS + 4 * i + d, 8 * k : 8 * k + 8, :] for k in range(3)]
                moved = [pltpu.roll(got[k], 32 + 32 * k, 1) for k in range(3)]
                parts += got
                parts.append(jnp.where(lane < 32, moved[0], jnp.where(lane < 64, moved[1], moved[2])))
            block = jnp.transpose(jnp.concatenate(parts, axis=0))[: 2 * WIN]
            spot = pl.ds(pl.multiple_of(2 * WIN * i, 8), 2 * WIN)
            mid[spot, :] = fine_dot(block, inv_ref[...])
            return carry

        lax.fori_loop(0, 16, unpack, 0)

        def finish(g, carry):
            def load(m):
                spot = pl.ds(pl.multiple_of(WIN * m + 8 * g, 8), 8)
                return mid[spot, 0:128], mid[spot, 128:256]

            values = inverse_outer(load, OUTER, turn_ref)

            def spot(t):
                return pl.ds(pl.multiple_of(WIN * t + 8 * g, 8), 8)

            if q == 0:
                for t in range(OUTER):
                    near[2, spot(t), :] = values[t]
                for d in (-2, -1, 1, 2):
                    moved = [pltpu.roll(v, (-d) % 128, 1) for v in values]
                    for t in range(OUTER):
                        if d < 0:
                            v = jnp.where(lane < -d, moved[t - 1], moved[t])
                        else:
                            v = jnp.where(lane < 128 - d, moved[t], moved[(t + 1) % OUTER])
                        near[2 + d, spot(t), :] = v
            else:
                moved = [pltpu.roll(v, 32, 1) for v in values]
                for t in range(OUTER):
                    even[spot(t), :] = jnp.where(lane < 32, moved[t - 1], moved[t])
                moved = [pltpu.roll(v, 96, 1) for v in values]
                for t in range(OUTER):
                    odd[spot(t), :] = jnp.where(lane < 96, moved[t], moved[(t + 1) % OUTER])
            return carry

        lax.fori_loop(0, WIN // 8, finish, 0)

    def tile(t, carry):
        cols = pl.ds(pl.multiple_of(128 * t, 128), 128)
        off_y = off_ref[0, :, cols]
        off_x = off_ref[1, :, cols]
        rel_y = 4.0 * off_y
        low_y = jnp.minimum(jnp.floor(rel_y), 1.0)
        left = off_x < 0.0
        frac_x = jnp.where(left, off_x + 1.0, off_x)
        bits = [low_y >= 0.0, (low_y == -1.0) | (low_y == 1.0)]
        taps = []
        for c in range(4):
            cells = []
            for j in range(4, 11):
                rows = pl.ds(WIN * t + j, 8, stride=4)
                cells.append(jnp.where(left, near[c, rows, :], near[c + 1, rows, :]))
            cells = [jnp.where(bits[0], cells[k + 2], cells[k]) for k in range(5)]
            taps.append([jnp.where(bits[1], cells[k + 1], cells[k]) for k in range(4)])
        first = stencil(taps, spline_weights(frac_x), spline_weights(rel_y - low_y))
        pos_y = (7.0 + rel_y) - lens_ratio * first[0]
        start = (32 + lax.rem(lane, 64)).astype(jnp.float32)
        pos_x = (start + off_x) - lens_ratio * first[1]
        low_y = jnp.floor(pos_y)
        low_x = jnp.floor(pos_x)
        cell_x = jnp.clip(low_x, -8.0, 136.0).astype(jnp.int32) - 1
        cell_y = jnp.clip(low_y, -8.0, 32.0).astype(jnp.int32) - 1
        xw = kept(spline_weights(pos_x - low_x), cell_x, 128)
        yw = kept(spline_weights(pos_y - low_y), cell_y, PATCH_ROWS)
        is_even = lane < 64
        bits = [(cell_y & b) != 0 for b in (8, 4, 2, 1)]
        taps = []
        for c in range(4):
            spots = jnp.clip(cell_x + c, 0, 127)
            cells = []
            for j in range(PATCH_ROWS):
                rows = pl.ds(WIN * t + j, 8, stride=4)
                cells.append(
                    jnp.where(is_even, lane_gather(even[rows, :], spots), lane_gather(odd[rows, :], spots))
                )
            cells = [jnp.where(bits[0], cells[(k + 8) % 16], cells[k]) for k in range(11)]
            cells = [jnp.where(bits[1], cells[k + 4], cells[k]) for k in range(7)]
            cells = [jnp.where(bits[2], cells[k + 2], cells[k]) for k in range(5)]
            taps.append([jnp.where(bits[3], cells[k + 1], cells[k]) for k in range(4)])
        second = stencil(taps, xw, yw)
        hess_yy, hess_xx, hess_xy = first[2], first[3], first[4]
        other_yy, other_xx, other_xy = second[2], second[3], second[4]
        lensed_yy = 1.0 - lens_ratio * hess_yy
        lensed_xx = 1.0 - lens_ratio * hess_xx
        lensed_xy = -lens_ratio * hess_xy
        deflect_ref[0, :, cols] = first[0] + second[0]
        deflect_ref[1, :, cols] = first[1] + second[1]
        jacob_ref[0, :, cols] = 1.0 - hess_yy - (other_yy * lensed_yy + other_xy * lensed_xy)
        jacob_ref[1, :, cols] = -hess_xy - (other_yy * lensed_xy + other_xy * lensed_xx)
        jacob_ref[2, :, cols] = -hess_xy - (other_xy * lensed_yy + other_xx * lensed_xy)
        jacob_ref[3, :, cols] = 1.0 - hess_xx - (other_xy * lensed_xy + other_xx * lensed_xx)
        return carry

    lax.fori_loop(0, OUTER, tile, 0, unroll=UNROLL)


def vmem(shape):
    return pltpu.VMEM(shape, jnp.float32)


def call(kernel, name, args, outs, scratch):
    return pl.pallas_call(
        kernel,
        name=name,
        out_shape=outs,
        in_specs=[pl.BlockSpec(memory_space=pltpu.VMEM)] * len(args),
        out_specs=jax.tree.map(lambda _: pl.BlockSpec(memory_space=pltpu.VMEM), outs),
        scratch_shapes=scratch,
        compiler_params=pltpu.CompilerParams(vmem_limit_bytes=60 * 1024 * 1024),
    )(*args)


def shape(*dims):
    return jax.ShapeDtypeStruct(dims, jnp.float32)


def on_device(kappa, ray_offsets):
    tab = tables()
    spectra = call(
        rows_kernel, "rows", (kappa[0], tab["row_fwd"], tab["row_turn"]), shape(2048, 128), [vmem((2048, 256))]
    )
    columns = lax.all_to_all(spectra.reshape(SLABS, 32, 128), "slab", split_axis=0, concat_axis=0, tiled=True)
    strips = call(
        columns_kernel,
        "columns",
        (columns, tab["col_fwd"], tab["col_turn"], tab["wave2"], tab["col_inv"], tab["col_back"]),
        shape(2 * SLABS, 24, 128),
        [vmem((512, 256)), vmem((512, 128)), vmem((2 * SLABS, 32, 128))],
    )
    windows = lax.all_to_all(strips, ("plane", "slab"), split_axis=0, concat_axis=0, tiled=True)
    deflection, jacobian = call(
        rays_kernel,
        "rays",
        (windows, tab["row_inv"], tab["row_turn"], ray_offsets[:, 0, 0]),
        (shape(2, 8, N), shape(4, 8, N)),
        [vmem((OUTER * WIN, 256)), vmem((5, OUTER * WIN, 128)), vmem((OUTER * WIN, 128)), vmem((OUTER * WIN, 128))],
    )
    return deflection[:, None, None], jacobian[:, None, None]


def solution(mesh):
    placed = (P("plane", "slab", None), P(None, "slab", "plane", None, None))
    return jax.shard_map(
        on_device,
        mesh=mesh,
        in_specs=placed,
        out_specs=(P(None, "slab", "plane", None, None), P(None, "slab", "plane", None, None)),
        check_vma=False,
    )
```

```python
import functools
import math

import jax
import jax.numpy as jnp
import numpy as np
from jax import lax
from jax.experimental import pallas as pl
from jax.experimental.pallas import tpu as pltpu
from jax.sharding import PartitionSpec as P

N = 4096
OUTER = 32
SLABS = 64
PATCH_ROWS = 16
WIN = 48
LEAD = 5
lens_ratio = 0.5
screen_modes = 4.0


def angles(left, right, length):
    return (np.outer(left, right) % length) * (2.0 * np.pi / length)


def cas_pair(left, right, length):
    a = angles(left, right, length)
    return np.cos(a) + np.sin(a), np.cos(a) - np.sin(a)


def f32(table):
    return np.asarray(table, np.float32)


def parts(table, count):
    out = []
    for _ in range(count):
        out.append(np.asarray(table, jnp.bfloat16))
        table = table - np.asarray(out[-1], np.float64)
    return out


@functools.cache
def tables():
    out = {}
    lane = np.arange(128)
    plus, minus = cas_pair(lane, lane, 128)
    out["row_fwd"] = np.concatenate(parts(np.concatenate([plus.T, minus.T], axis=1), 2), axis=0)
    turn = angles(np.arange(OUTER), lane, N)
    out["row_turn"] = f32(np.stack([np.cos(turn), np.sin(turn)]))
    out["row_inv"] = np.stack(parts(0.5 * np.concatenate([plus, -minus], axis=1), 3))
    sixty = np.arange(64)
    plus, minus = cas_pair(sixty, sixty, 64)
    two = np.eye(2)
    both = np.concatenate([np.kron(two, plus), np.kron(two, minus)], axis=0)
    out["col_fwd"] = np.concatenate(parts(both, 2), axis=1)
    turn = angles(sixty, np.concatenate([sixty, sixty]), N)
    out["col_turn"] = f32(np.stack([np.cos(turn), np.sin(turn)]))
    inv, turns = [], []
    for p in range(2):
        rows = 32 * p - LEAD + np.arange(WIN)
        plus, minus = cas_pair(sixty, rows, 64)
        pad = np.zeros((128, 32))
        inv.append(np.concatenate([np.kron(two, plus), pad, -np.kron(two, minus), pad], axis=1))
        turn = angles(sixty, np.concatenate([rows, rows, np.zeros(32, rows.dtype)]), N)
        turns.append(np.stack([np.cos(turn), np.sin(turn)]))
    out["col_inv"] = np.stack([np.stack(parts(0.5 * table, 3)) for table in inv])
    out["col_back"] = f32(np.stack(turns))
    ids = np.arange(64)[:, None] + 64 * np.concatenate([sixty, sixty])[None, :]
    wave = 2.0 * np.pi / N * np.minimum(ids, N - ids)
    out["wave2"] = f32(wave**2)
    return out


def cmul(re, im, c, s):
    if abs(s) < 1e-12 and abs(c - 1.0) < 1e-12:
        return re, im
    if abs(c) < 1e-12 and abs(s - 1.0) < 1e-12:
        return (None if im is None else -im), re
    if im is None:
        return re * c, re * s
    if re is None:
        return im * (-s), im * c
    if abs(c - s) < 1e-12:
        return (re - im) * c, (re + im) * c
    if abs(c + s) < 1e-12:
        return (re + im) * c, (im - re) * c
    return re * c - im * s, re * s + im * c


def add(a, b):
    return b if a is None else a if b is None else a + b


def sub(a, b):
    return a if b is None else -b if a is None else a - b


def neg(a):
    return None if a is None else -a


def real_to_half(xs):
    n = len(xs)
    if n == 2:
        return [(xs[0] + xs[1], None), (xs[0] - xs[1], None)]
    even, odd = real_to_half(xs[0::2]), real_to_half(xs[1::2])
    half = n // 2
    out = [None] * (half + 1)
    for k in range(half // 2 + 1):
        c, s = math.cos(2 * math.pi * k / n), math.sin(2 * math.pi * k / n)
        tr, ti = cmul(*odd[k], c, s)
        er, ei = even[k]
        out[k] = (add(er, tr), add(ei, ti))
        if half - k != k:
            out[half - k] = (sub(er, tr), sub(ti, ei))
    return out


def half_to_real(xs):
    half = len(xs) - 1
    n = 2 * half
    if n == 2:
        return [xs[0][0] + xs[1][0], xs[0][0] - xs[1][0]]
    even, odd = [], []
    for k in range(half // 2 + 1):
        ar, ai = xs[k]
        br, bi = xs[half - k]
        if k == half - k:
            even.append((ar + ar, None))
            odd.append((-(ai + ai), None))
            continue
        even.append((add(ar, br), sub(ai, bi)))
        c, s = math.cos(2 * math.pi * k / n), math.sin(2 * math.pi * k / n)
        odd.append(cmul(sub(ar, br), add(ai, bi), c, s))
    evens, odds = half_to_real(even), half_to_real(odd)
    return [v for pair in zip(evens, odds) for v in pair]


def row8(ref, *index):
    return jnp.broadcast_to(ref[index], (8, 128))


def turned(re, im, c, s):
    if im is None:
        return re * c, re * s
    return re * c - im * s, re * s + im * c


def forward_outer(xs, turn_ref, store):
    n = len(xs)
    half = real_to_half(xs)
    for m in range(n):
        re, im = half[m] if m <= n // 2 else (half[n - m][0], neg(half[n - m][1]))
        store(m, *turned(re, im, row8(turn_ref, 0, slice(m, m + 1)), row8(turn_ref, 1, slice(m, m + 1))))


def inverse_outer(load, n, turn_ref, *lead):
    def value(m):
        re, im = load(m)
        return turned(re, im, row8(turn_ref, *lead, 0, slice(m, m + 1)), row8(turn_ref, *lead, 1, slice(m, m + 1)))

    spectrum = []
    for m in range(n // 2 + 1):
        re, im = value(m)
        if m in (0, n // 2):
            spectrum.append((re + re, None))
        else:
            ro, io = value(n - m)
            spectrum.append((re + ro, im - io))
    return half_to_real(spectrum)


def split(x, count):
    out = []
    for i in range(count):
        out.append(x.astype(jnp.bfloat16))
        if i + 1 < count:
            x = x - out[-1].astype(jnp.float32)
    return out


def fine_dot(x, w):
    a, b, c = split(x, 3)
    w0, w1, w2 = w[0], w[1], w[2]
    left = jnp.concatenate([a, b, a, b, a, c], axis=1)
    right = jnp.concatenate([w0, w0, w1, w1, w2, w0], axis=0)
    return jnp.dot(left, right, preferred_element_type=jnp.float32)


def rows_kernel(kappa_ref, weight_ref, turn_ref, out_ref, mid):
    def group(g, carry):
        rows = pl.ds(pl.multiple_of(8 * g, 8), 8)
        xs = [kappa_ref[rows, 128 * j : 128 * j + 128] for j in range(OUTER)]

        def store(m, re, im):
            spot = pl.ds(pl.multiple_of(64 * m + 8 * g, 8), 8)
            mid[spot, 0:128] = re
            mid[spot, 128:256] = im

        forward_outer(xs, turn_ref, store)
        return carry

    lax.fori_loop(0, 8, group, 0, unroll=2)

    def pair(i, carry):
        spot = pl.ds(pl.multiple_of(128 * i, 128), 128)
        left = jnp.concatenate([weight_ref[...]] * 2, axis=1)
        right = jnp.concatenate(split(mid[spot, :], 2), axis=1)
        both = lax.dot_general(left, right, (((1,), (1,)), ((), ())), preferred_element_type=jnp.float32)
        out_ref[spot, :] = both[:128] + both[128:]
        return carry

    lax.fori_loop(0, 16, pair, 0, unroll=8)


def columns_kernel(in_ref, fwd_ref, turn_ref, wave_ref, inv_ref, back_ref, out_ref, mid, spec, strips):
    owner = lax.axis_index("slab")
    base = 2 * lax.div(owner, 4) + 1024 * lax.rem(owner, 4)
    lane = lax.broadcasted_iota(jnp.int32, (8, 128), 1)
    sub8 = lax.broadcasted_iota(jnp.int32, (8, 128), 0)
    screen = (2.0 * math.pi * screen_modes / N) ** 2

    def group(g, carry):
        rows = pl.ds(pl.multiple_of(8 * g, 8), 8)
        xs = [in_ref[s, rows, :] for s in range(SLABS)]

        def store(m, re, im):
            mid[8 * m : 8 * m + 8, 0:128] = re
            mid[8 * m : 8 * m + 8, 128:256] = im

        forward_outer(xs, turn_ref, store)
        left = jnp.concatenate(split(mid[...], 2), axis=1)
        right = jnp.concatenate([fwd_ref[...]] * 2, axis=0)
        both = jnp.dot(left, right, preferred_element_type=jnp.float32)
        spec[...] = both[:, :128] + both[:, 128:]
        ids = base + jnp.where(lane >= 64, 1, 0) + 32 * (8 * g + sub8)
        wave = (2.0 * math.pi / N) * jnp.minimum(ids, N - ids).astype(jnp.float32)
        mine = wave * wave + screen
        for m in range(SLABS):
            factor = -2.0 / ((mine + row8(wave_ref, slice(m, m + 1))) * float(N * N))
            if m == 0:
                factor = jnp.where((ids == 0) & (lane == 0), 0.0, factor)
            spec[8 * m : 8 * m + 8, :] = spec[8 * m : 8 * m + 8, :] * factor
        for p in range(2):
            mid[...] = fine_dot(spec[...], inv_ref[p])
            values = inverse_outer(
                lambda m: (mid[8 * m : 8 * m + 8, 0:128], mid[8 * m : 8 * m + 8, 128:256]), SLABS, back_ref, p
            )
            for s in range(SLABS):
                strips[p * SLABS + s, rows, :] = values[s]
        return carry

    lax.fori_loop(0, 4, group, 0)

    def pack(d, carry):
        last = strips[d, 24:32, :]
        for k in range(3):
            moved = last if k == 3 else pltpu.roll(last, (96 - 32 * k) % 128, 1)
            out_ref[d, 8 * k : 8 * k + 8, :] = jnp.where(lane < 96, strips[d, 8 * k : 8 * k + 8, :], moved)
        return carry

    lax.fori_loop(0, 2 * SLABS, pack, 0, unroll=32)


def spline_weights(f):
    e = 1.0 - f
    f2, e2 = f * f, e * e
    f3, e3 = f2 * f, e2 * e
    sixth, third = 1.0 / 6.0, 2.0 / 3.0
    value = [e3 * sixth, third - f2 + 0.5 * f3, third - e2 + 0.5 * e3, f3 * sixth]
    slope = [-0.5 * e2, 1.5 * f2 - 2.0 * f, 2.0 * e - 1.5 * e2, 0.5 * f2]
    curve = [e, 3.0 * f - 2.0, 1.0 - 3.0 * f, f]
    return value, slope, curve


def dot4(ws, vs):
    return (ws[0] * vs[0] + ws[1] * vs[1]) + (ws[2] * vs[2] + ws[3] * vs[3])


def stencil(taps, xw, yw):
    rows = list(zip(*taps))
    flat = [dot4(xw[0], row) for row in rows]
    slope = [dot4(xw[1], row) for row in rows]
    curve = [dot4(xw[2], row) for row in rows]
    return dot4(yw[1], flat), dot4(yw[0], slope), dot4(yw[2], flat), dot4(yw[0], curve), dot4(yw[1], slope)


def kept(weights, first, count):
    inside = [(first + c >= 0) & (first + c < count) for c in range(4)]
    return [[jnp.where(inside[c], w[c], 0.0) for c in range(4)] for w in weights]


def lane_gather(values, spots):
    dims = lax.GatherDimensionNumbers(
        offset_dims=(), collapsed_slice_dims=(1,), start_index_map=(1,),
        operand_batching_dims=(0,), start_indices_batching_dims=(0,),
    )
    return lax.gather(
        values, spots[..., None], dims, (1, 1), mode=lax.GatherScatterMode.PROMISE_IN_BOUNDS
    )


def rays_kernel(in_ref, inv_ref, turn_ref, off_ref, deflect_ref, jacob_ref, mid, near, even, odd):
    lane = lax.broadcasted_iota(jnp.int32, (8, 128), 1)

    for q in range(2):
        def unpack(i, carry):
            parts = []
            for d in range(4):
                got = [in_ref[q * SLABS + 4 * i + d, 8 * k : 8 * k + 8, :] for k in range(3)]
                moved = [pltpu.roll(got[k], 32 + 32 * k, 1) for k in range(3)]
                parts += got
                parts.append(jnp.where(lane < 32, moved[0], jnp.where(lane < 64, moved[1], moved[2])))
            block = jnp.transpose(jnp.concatenate(parts, axis=0))[: 2 * WIN]
            spot = pl.ds(pl.multiple_of(2 * WIN * i, 8), 2 * WIN)
            mid[spot, :] = fine_dot(block, inv_ref[...])
            return carry

        lax.fori_loop(0, 16, unpack, 0, unroll=8)

        def finish(g, carry):
            def load(m):
                spot = pl.ds(pl.multiple_of(WIN * m + 8 * g, 8), 8)
                return mid[spot, 0:128], mid[spot, 128:256]

            values = inverse_outer(load, OUTER, turn_ref)

            def spot(t):
                return pl.ds(pl.multiple_of(WIN * t + 8 * g, 8), 8)

            if q == 0:
                for t in range(OUTER):
                    near[2, spot(t), :] = values[t]
                for d in (-2, -1, 1, 2):
                    moved = [pltpu.roll(v, (-d) % 128, 1) for v in values]
                    for t in range(OUTER):
                        if d < 0:
                            v = jnp.where(lane < -d, moved[t - 1], moved[t])
                        else:
                            v = jnp.where(lane < 128 - d, moved[t], moved[(t + 1) % OUTER])
                        near[2 + d, spot(t), :] = v
            else:
                moved = [pltpu.roll(v, 32, 1) for v in values]
                for t in range(OUTER):
                    even[spot(t), :] = jnp.where(lane < 32, moved[t - 1], moved[t])
                moved = [pltpu.roll(v, 96, 1) for v in values]
                for t in range(OUTER):
                    odd[spot(t), :] = jnp.where(lane < 96, moved[t], moved[(t + 1) % OUTER])
            return carry

        lax.fori_loop(0, WIN // 8, finish, 0, unroll=3)

    def tile(t, carry):
        cols = pl.ds(pl.multiple_of(128 * t, 128), 128)
        off_y = off_ref[0, :, cols]
        off_x = off_ref[1, :, cols]
        rel_y = 4.0 * off_y
        low_y = jnp.minimum(jnp.floor(rel_y), 1.0)
        left = off_x < 0.0
        frac_x = jnp.where(left, off_x + 1.0, off_x)
        bits = [low_y >= 0.0, (low_y == -1.0) | (low_y == 1.0)]
        taps = []
        for c in range(4):
            cells = []
            for j in range(4, 11):
                rows = pl.ds(WIN * t + j, 8, stride=4)
                cells.append(jnp.where(left, near[c, rows, :], near[c + 1, rows, :]))
            cells = [jnp.where(bits[0], cells[k + 2], cells[k]) for k in range(5)]
            taps.append([jnp.where(bits[1], cells[k + 1], cells[k]) for k in range(4)])
        first = stencil(taps, spline_weights(frac_x), spline_weights(rel_y - low_y))
        pos_y = (7.0 + rel_y) - lens_ratio * first[0]
        start = (32 + lax.rem(lane, 64)).astype(jnp.float32)
        pos_x = (start + off_x) - lens_ratio * first[1]
        low_y = jnp.floor(pos_y)
        low_x = jnp.floor(pos_x)
        cell_x = jnp.clip(low_x, -8.0, 136.0).astype(jnp.int32) - 1
        cell_y = jnp.clip(low_y, -8.0, 32.0).astype(jnp.int32) - 1
        xw = kept(spline_weights(pos_x - low_x), cell_x, 128)
        yw = kept(spline_weights(pos_y - low_y), cell_y, PATCH_ROWS)
        is_even = lane < 64
        bits = [(cell_y & b) != 0 for b in (8, 4, 2, 1)]
        taps = []
        for c in range(4):
            spots = jnp.clip(cell_x + c, 0, 127)
            cells = []
            for j in range(PATCH_ROWS):
                rows = pl.ds(WIN * t + j, 8, stride=4)
                cells.append(
                    jnp.where(is_even, lane_gather(even[rows, :], spots), lane_gather(odd[rows, :], spots))
                )
            cells = [jnp.where(bits[0], cells[(k + 8) % 16], cells[k]) for k in range(11)]
            cells = [jnp.where(bits[1], cells[k + 4], cells[k]) for k in range(7)]
            cells = [jnp.where(bits[2], cells[k + 2], cells[k]) for k in range(5)]
            taps.append([jnp.where(bits[3], cells[k + 1], cells[k]) for k in range(4)])
        second = stencil(taps, xw, yw)
        hess_yy, hess_xx, hess_xy = first[2], first[3], first[4]
        other_yy, other_xx, other_xy = second[2], second[3], second[4]
        lensed_yy = 1.0 - lens_ratio * hess_yy
        lensed_xx = 1.0 - lens_ratio * hess_xx
        lensed_xy = -lens_ratio * hess_xy
        deflect_ref[0, :, cols] = first[0] + second[0]
        deflect_ref[1, :, cols] = first[1] + second[1]
        jacob_ref[0, :, cols] = 1.0 - hess_yy - (other_yy * lensed_yy + other_xy * lensed_xy)
        jacob_ref[1, :, cols] = -hess_xy - (other_yy * lensed_xy + other_xy * lensed_xx)
        jacob_ref[2, :, cols] = -hess_xy - (other_xy * lensed_yy + other_xx * lensed_xy)
        jacob_ref[3, :, cols] = 1.0 - hess_xx - (other_xy * lensed_xy + other_xx * lensed_xx)
        return carry

    lax.fori_loop(0, OUTER, tile, 0, unroll=4)


def vmem(shape):
    return pltpu.VMEM(shape, jnp.float32)


def call(kernel, name, args, outs, scratch, limit=16):
    return pl.pallas_call(
        kernel,
        name=name,
        out_shape=outs,
        in_specs=[pl.BlockSpec(memory_space=pltpu.VMEM)] * len(args),
        out_specs=jax.tree.map(lambda _: pl.BlockSpec(memory_space=pltpu.VMEM), outs),
        scratch_shapes=scratch,
        compiler_params=pltpu.CompilerParams(vmem_limit_bytes=limit * 1024 * 1024),
    )(*args)


def shape(*dims):
    return jax.ShapeDtypeStruct(dims, jnp.float32)


def on_device(kappa, ray_offsets):
    tab = tables()
    spectra = call(
        rows_kernel, "rows", (kappa[0], tab["row_fwd"], tab["row_turn"]), shape(2048, 128), [vmem((2048, 256))]
    )
    columns = lax.all_to_all(spectra.reshape(SLABS, 32, 128), "slab", split_axis=0, concat_axis=0, tiled=True)
    strips = call(
        columns_kernel,
        "columns",
        (columns, tab["col_fwd"], tab["col_turn"], tab["wave2"], tab["col_inv"], tab["col_back"]),
        shape(2 * SLABS, 24, 128),
        [vmem((512, 256)), vmem((512, 128)), vmem((2 * SLABS, 32, 128))],
    )
    windows = lax.all_to_all(strips, ("plane", "slab"), split_axis=0, concat_axis=0, tiled=True)
    deflection, jacobian = call(
        rays_kernel,
        "rays",
        (windows, tab["row_inv"], tab["row_turn"], ray_offsets[:, 0, 0]),
        (shape(2, 8, N), shape(4, 8, N)),
        [vmem((OUTER * WIN, 256)), vmem((5, OUTER * WIN, 128)), vmem((OUTER * WIN, 128)), vmem((OUTER * WIN, 128))],
    )
    return deflection[:, None, None], jacobian[:, None, None]


def solution(mesh):
    placed = (P("plane", "slab", None), P(None, "slab", "plane", None, None))
    return jax.shard_map(
        on_device,
        mesh=mesh,
        in_specs=placed,
        out_specs=(P(None, "slab", "plane", None, None), P(None, "slab", "plane", None, None)),
        check_vma=False,
    )
```

```python
import functools
import math

import jax
import jax.numpy as jnp
import numpy as np
from jax import lax
from jax.experimental import pallas as pl
from jax.experimental.pallas import tpu as pltpu
from jax.sharding import PartitionSpec as P

N = 4096
OUTER = 32
SLABS = 64
PATCH_ROWS = 16
NEAR_WIN = 40
WIN = 48
ROWS_GRANT = 62 * 1024 * 1024
LEAD = 5
lens_ratio = 0.5
screen_modes = 4.0


def angles(left, right, length):
    return (np.outer(left, right) % length) * (2.0 * np.pi / length)


def cas_pair(left, right, length):
    a = angles(left, right, length)
    return np.cos(a) + np.sin(a), np.cos(a) - np.sin(a)


def f32(table):
    return np.asarray(table, np.float32)


def parts(table, count):
    out = []
    for _ in range(count):
        out.append(np.asarray(table, jnp.bfloat16))
        table = table - np.asarray(out[-1], np.float64)
    return out


@functools.cache
def tables():
    out = {}
    lane = np.arange(128)
    plus, minus = cas_pair(lane, lane, 128)
    both = np.concatenate([plus, minus], axis=0)
    out["row_fwd"] = np.concatenate(parts(both, 2), axis=1)
    turn = angles(np.arange(OUTER), lane, N)
    out["row_turn"] = f32(np.stack([np.cos(turn), np.sin(turn)]))
    out["row_inv"] = np.stack(parts(0.5 * np.concatenate([plus, -minus], axis=1), 3))
    sixty = np.arange(64)
    plus, minus = cas_pair(sixty, sixty, 64)
    two = np.eye(2)
    both = np.concatenate([np.kron(two, plus), np.kron(two, minus)], axis=0)
    out["col_fwd"] = np.concatenate(parts(both, 2), axis=1)
    turn = angles(sixty, np.concatenate([sixty, sixty]), N)
    out["col_turn"] = f32(np.stack([np.cos(turn), np.sin(turn)]))
    inv, extra, turns = [], [], []
    for p in range(2):
        rows = 32 * p - LEAD + np.arange(WIN)
        plus, minus = cas_pair(sixty, rows, 64)
        table = 0.5 * np.stack([np.kron(two, plus), -np.kron(two, minus)], axis=1)
        turn = angles(sixty, np.concatenate([rows, rows]), N)
        inv.append(np.pad(table, ((0, 0), (0, 0), (0, 32))).reshape(128, 256))
        for k in range(3):
            own = slice(32 * k, 32 * k + 32)
            extra.append(np.pad(table[:, :, own], ((0, 0), (0, 0), (96, 0))).reshape(128, 256))
            full = np.concatenate([turn, turn[:, own]], axis=1)
            turns.append(np.stack([np.cos(full), np.sin(full)]))
    out["col_inv"] = np.stack([np.stack(parts(table, 3)) for table in inv])
    out["col_extra"] = np.stack([np.stack(parts(table, 3)) for table in extra]).reshape(2, 3, 3, 128, 256)
    out["col_back"] = f32(np.stack(turns).reshape(2, 3, 2, 64, 128))
    ids = np.arange(64)[:, None] + 64 * np.concatenate([sixty, sixty])[None, :]
    wave = 2.0 * np.pi / N * np.minimum(ids, N - ids)
    out["wave2"] = f32(wave**2)
    return out


def cmul(re, im, c, s):
    if abs(s) < 1e-12 and abs(c - 1.0) < 1e-12:
        return re, im
    if abs(c) < 1e-12 and abs(s - 1.0) < 1e-12:
        return (None if im is None else -im), re
    if im is None:
        return re * c, re * s
    if re is None:
        return im * (-s), im * c
    if abs(c - s) < 1e-12:
        return (re - im) * c, (re + im) * c
    if abs(c + s) < 1e-12:
        return (re + im) * c, (im - re) * c
    return re * c - im * s, re * s + im * c


def add(a, b):
    return b if a is None else a if b is None else a + b


def sub(a, b):
    return a if b is None else -b if a is None else a - b


def neg(a):
    return None if a is None else -a


def real_to_half(xs):
    n = len(xs)
    if n == 2:
        return [(xs[0] + xs[1], None), (xs[0] - xs[1], None)]
    even, odd = real_to_half(xs[0::2]), real_to_half(xs[1::2])
    half = n // 2
    out = [None] * (half + 1)
    for k in range(half // 2 + 1):
        c, s = math.cos(2 * math.pi * k / n), math.sin(2 * math.pi * k / n)
        tr, ti = cmul(*odd[k], c, s)
        er, ei = even[k]
        out[k] = (add(er, tr), add(ei, ti))
        if half - k != k:
            out[half - k] = (sub(er, tr), sub(ti, ei))
    return out


def half_to_real(xs):
    half = len(xs) - 1
    n = 2 * half
    if n == 2:
        return [xs[0][0] + xs[1][0], xs[0][0] - xs[1][0]]
    even, odd = [], []
    for k in range(half // 2 + 1):
        ar, ai = xs[k]
        br, bi = xs[half - k]
        if k == half - k:
            even.append((ar + ar, None))
            odd.append((-(ai + ai), None))
            continue
        even.append((add(ar, br), sub(ai, bi)))
        c, s = math.cos(2 * math.pi * k / n), math.sin(2 * math.pi * k / n)
        odd.append(cmul(sub(ar, br), add(ai, bi), c, s))
    evens, odds = half_to_real(even), half_to_real(odd)
    return [v for pair in zip(evens, odds) for v in pair]


def row8(ref, *index):
    return jnp.broadcast_to(ref[index], (8, 128))


def turned(re, im, c, s):
    if im is None:
        return re * c, re * s
    return re * c - im * s, re * s + im * c


def forward_outer(xs, turn_ref, store):
    n = len(xs)
    half = real_to_half(xs)
    for m in range(n):
        re, im = half[m] if m <= n // 2 else (half[n - m][0], neg(half[n - m][1]))
        store(m, *turned(re, im, row8(turn_ref, 0, slice(m, m + 1)), row8(turn_ref, 1, slice(m, m + 1))))


def inverse_outer(load, n, turn_ref, *lead):
    def value(m):
        re, im = load(m)
        return turned(re, im, row8(turn_ref, *lead, 0, slice(m, m + 1)), row8(turn_ref, *lead, 1, slice(m, m + 1)))

    spectrum = []
    for m in range(n // 2 + 1):
        re, im = value(m)
        if m in (0, n // 2):
            spectrum.append((re + re, None))
        else:
            ro, io = value(n - m)
            spectrum.append((re + ro, im - io))
    return half_to_real(spectrum)


def split(x, count):
    out = []
    for i in range(count):
        out.append(x.astype(jnp.bfloat16))
        if i + 1 < count:
            x = x - out[-1].astype(jnp.float32)
    return out


def left_of(pieces):
    a, b, c = (pieces[:, 128 * i : 128 * i + 128] for i in range(3))
    return [a, b, a, b, a, c]


def right_of(w):
    return [w[0], w[0], w[1], w[1], w[2], w[0]]


def fine_dot(x, w):
    left = jnp.concatenate(left_of(jnp.concatenate(split(x, 3), axis=1)), axis=1)
    return jnp.dot(left, jnp.concatenate(right_of(w), axis=0), preferred_element_type=jnp.float32)


def coarse_dot(x, w):
    left = jnp.concatenate(split(x, 2), axis=1)
    both = jnp.dot(left, jnp.concatenate([w, w], axis=0), preferred_element_type=jnp.float32)
    return both[:, :128] + both[:, 128:]


def rows_kernel(kappa_hbm, weight_hbm, turn_hbm, out_hbm, out_ref, kappa_ref, weight_ref, turn_ref, mid, sems):
    def fetch(g):
        rows = pl.ds(8 * g, 8)
        return pltpu.make_async_copy(kappa_hbm.at[rows, :], kappa_ref.at[rows, :], sems.at[g])

    def send(i):
        rows = pl.ds(512 * i, 512)
        return pltpu.make_async_copy(out_ref.at[rows, :], out_hbm.at[rows, :], sems.at[10 + i])

    turn_copy = pltpu.make_async_copy(turn_hbm, turn_ref, sems.at[8])
    weight_copy = pltpu.make_async_copy(weight_hbm, weight_ref, sems.at[9])
    turn_copy.start()
    for g in range(8):
        fetch(g).start()
    weight_copy.start()
    turn_copy.wait()
    for g in range(8):
        fetch(g).wait()
        xs = [kappa_ref[8 * g : 8 * g + 8, 128 * j : 128 * j + 128] for j in range(OUTER)]

        def store(m, re, im):
            mid[64 * m + 8 * g : 64 * m + 8 * g + 8, 0:128] = re
            mid[64 * m + 8 * g : 64 * m + 8 * g + 8, 128:256] = im

        forward_outer(xs, turn_ref, store)
    weight_copy.wait()
    for i in range(4):
        found = coarse_dot(mid[512 * i : 512 * i + 512, :], weight_ref[...])
        for k in range(4):
            out_ref[512 * i + 128 * k : 512 * i + 128 * k + 128, :] = jnp.transpose(found[128 * k : 128 * k + 128])
        send(i).start()
    for i in range(4):
        send(i).wait()


def columns_kernel(in_ref, fwd_ref, turn_ref, wave_ref, inv_ref, extra_ref, back_ref, out_ref, mids, specs, pieces):
    owner = lax.axis_index("slab")
    base = 2 * lax.div(owner, 4) + 1024 * lax.rem(owner, 4)
    lane = lax.broadcasted_iota(jnp.int32, (8, 128), 1)
    sub8 = lax.broadcasted_iota(jnp.int32, (8, 128), 0)
    screen = (2.0 * math.pi * screen_modes / N) ** 2

    def forward(g, mid, spec):
        rows = pl.ds(pl.multiple_of(8 * g, 8), 8)
        xs = [in_ref[s, rows, :] for s in range(SLABS)]

        def store(m, re, im):
            mid[8 * m : 8 * m + 8, 0:128] = re
            mid[8 * m : 8 * m + 8, 128:256] = im

        forward_outer(xs, turn_ref, store)
        spec[...] = coarse_dot(mid[...], fwd_ref[...])
        ids = base + jnp.where(lane >= 64, 1, 0) + 32 * (8 * g + sub8)
        wave = (2.0 * math.pi / N) * jnp.minimum(ids, N - ids).astype(jnp.float32)
        mine = wave * wave + screen
        for m in range(SLABS):
            factor = -2.0 / ((mine + row8(wave_ref, slice(m, m + 1))) * float(N * N))
            if m == 0:
                factor = jnp.where((ids == 0) & (lane == 0), 0.0, factor)
            spec[8 * m : 8 * m + 8, :] = spec[8 * m : 8 * m + 8, :] * factor
        for i, piece in enumerate(split(spec[...], 3)):
            pieces[g, :, 128 * i : 128 * i + 128] = piece

    def forward_pair(i, carry):
        forward(2 * i, mids.at[0], specs.at[0])
        forward(2 * i + 1, mids.at[1], specs.at[1])
        return carry

    lax.fori_loop(0, 2, forward_pair, 0, unroll=2)

    def backward(k, carry):
        for p in range(2):
            mid = mids.at[p]
            left = left_of(pieces[k]) + left_of(pieces[3])
            right = right_of(inv_ref[p]) + right_of(extra_ref[p, k])
            mid[...] = jnp.dot(
                jnp.concatenate(left, axis=1), jnp.concatenate(right, axis=0), preferred_element_type=jnp.float32
            )
            values = inverse_outer(
                lambda m: (mid[8 * m : 8 * m + 8, 0:128], mid[8 * m : 8 * m + 8, 128:256]), SLABS, back_ref, p, k
            )
            rows = pl.ds(pl.multiple_of(8 * k, 8), 8)
            for s in range(SLABS):
                out_ref[p * SLABS + s, rows, :] = values[s]
        return carry

    lax.fori_loop(0, 3, backward, 0, unroll=3)


def spline_weights(f):
    e = 1.0 - f
    f2, e2 = f * f, e * e
    f3, e3 = f2 * f, e2 * e
    sixth, third = 1.0 / 6.0, 2.0 / 3.0
    value = [e3 * sixth, third - f2 + 0.5 * f3, third - e2 + 0.5 * e3, f3 * sixth]
    slope = [-0.5 * e2, 1.5 * f2 - 2.0 * f, 2.0 * e - 1.5 * e2, 0.5 * f2]
    curve = [e, 3.0 * f - 2.0, 1.0 - 3.0 * f, f]
    return value, slope, curve


def dot4(ws, vs):
    return (ws[0] * vs[0] + ws[1] * vs[1]) + (ws[2] * vs[2] + ws[3] * vs[3])


def stencil(taps, xw, yw):
    rows = list(zip(*taps))
    flat = [dot4(xw[0], row) for row in rows]
    slope = [dot4(xw[1], row) for row in rows]
    curve = [dot4(xw[2], row) for row in rows]
    return dot4(yw[1], flat), dot4(yw[0], slope), dot4(yw[2], flat), dot4(yw[0], curve), dot4(yw[1], slope)


def kept(weights, first, count):
    inside = [(first + c >= 0) & (first + c < count) for c in range(4)]
    return [[jnp.where(inside[c], w[c], 0.0) for c in range(4)] for w in weights]


def lane_gather(values, spots):
    dims = lax.GatherDimensionNumbers(
        offset_dims=(), collapsed_slice_dims=(1,), start_index_map=(1,),
        operand_batching_dims=(0,), start_indices_batching_dims=(0,),
    )
    return lax.gather(
        values, spots[..., None], dims, (1, 1), mode=lax.GatherScatterMode.PROMISE_IN_BOUNDS
    )


def rays_kernel(
    in_ref, inv_ref, turn_ref, off_ref, deflect_hbm, jacob_hbm, deflect_ref, jacob_ref, flat, mid, near, even, odd, sems
):
    lane = lax.broadcasted_iota(jnp.int32, (8, 128), 1)

    for q, win in enumerate((NEAR_WIN, WIN)):
        def unpack(i, carry):
            rows = []
            for d in range(4):
                got = [in_ref[q * SLABS + 4 * i + d, 8 * k : 8 * k + 8, :] for k in range(3)]
                moved = [pltpu.roll(got[k], 32 + 32 * k, 1) for k in range(3)]
                rows += got
                rows.append(jnp.where(lane < 32, moved[0], jnp.where(lane < 64, moved[1], moved[2])))
            block = jnp.transpose(jnp.concatenate(rows, axis=0))
            for h in range(2):
                spot = pl.ds(pl.multiple_of(win * (2 * i + h), 8), win)
                flat[spot, :] = block[WIN * h : WIN * h + win]
            return carry

        lax.fori_loop(0, 16, unpack, 0, unroll=8)
        for half in (slice(0, 16 * win), slice(16 * win, 32 * win)):
            mid[half, :] = fine_dot(flat[half, :], inv_ref[...])

        def finish(g, carry):
            def load(m):
                spot = pl.ds(pl.multiple_of(win * m + 8 * g, 8), 8)
                return mid[spot, 0:128], mid[spot, 128:256]

            values = inverse_outer(load, OUTER, turn_ref)

            def spot(t):
                return pl.ds(pl.multiple_of(win * t + 8 * g, 8), 8)

            if q == 0:
                for t in range(OUTER):
                    near[2, spot(t), :] = values[t]
                for d in (-2, -1, 1, 2):
                    moved = [pltpu.roll(v, (-d) % 128, 1) for v in values]
                    for t in range(OUTER):
                        if d < 0:
                            v = jnp.where(lane < -d, moved[t - 1], moved[t])
                        else:
                            v = jnp.where(lane < 128 - d, moved[t], moved[(t + 1) % OUTER])
                        near[2 + d, spot(t), :] = v
            else:
                moved = [pltpu.roll(v, 32, 1) for v in values]
                for t in range(OUTER):
                    even[spot(t), :] = jnp.where(lane < 32, moved[t - 1], moved[t])
                moved = [pltpu.roll(v, 96, 1) for v in values]
                for t in range(OUTER):
                    odd[spot(t), :] = jnp.where(lane < 96, moved[t], moved[(t + 1) % OUTER])
            return carry

        lax.fori_loop(0, win // 8, finish, 0, unroll=5 if q == 0 else 3)

    def tile(t, carry):
        cols = pl.ds(pl.multiple_of(128 * t, 128), 128)
        off_y = off_ref[0, :, cols]
        off_x = off_ref[1, :, cols]
        rel_y = 4.0 * off_y
        low_y = jnp.minimum(jnp.floor(rel_y), 1.0)
        left = off_x < 0.0
        frac_x = jnp.where(left, off_x + 1.0, off_x)
        bits = [low_y >= 0.0, (low_y == -1.0) | (low_y == 1.0)]
        taps = []
        for c in range(4):
            cells = []
            for j in range(4, 11):
                rows = pl.ds(NEAR_WIN * t + j, 8, stride=4)
                cells.append(jnp.where(left, near[c, rows, :], near[c + 1, rows, :]))
            cells = [jnp.where(bits[0], cells[k + 2], cells[k]) for k in range(5)]
            taps.append([jnp.where(bits[1], cells[k + 1], cells[k]) for k in range(4)])
        first = stencil(taps, spline_weights(frac_x), spline_weights(rel_y - low_y))
        pos_y = (7.0 + rel_y) - lens_ratio * first[0]
        start = (32 + lax.rem(lane, 64)).astype(jnp.float32)
        pos_x = (start + off_x) - lens_ratio * first[1]
        low_y = jnp.floor(pos_y)
        low_x = jnp.floor(pos_x)
        cell_x = jnp.clip(low_x, -8.0, 136.0).astype(jnp.int32) - 1
        cell_y = jnp.clip(low_y, -8.0, 32.0).astype(jnp.int32) - 1
        xw = kept(spline_weights(pos_x - low_x), cell_x, 128)
        yw = kept(spline_weights(pos_y - low_y), cell_y, PATCH_ROWS)
        is_even = lane < 64
        bits = [(cell_y & b) != 0 for b in (8, 4, 2, 1)]
        taps = []
        for c in range(4):
            spots = jnp.clip(cell_x + c, 0, 127)
            cells = []
            for j in range(PATCH_ROWS):
                rows = pl.ds(WIN * t + j, 8, stride=4)
                cells.append(
                    jnp.where(is_even, lane_gather(even[rows, :], spots), lane_gather(odd[rows, :], spots))
                )
            cells = [jnp.where(bits[0], cells[(k + 8) % 16], cells[k]) for k in range(11)]
            cells = [jnp.where(bits[1], cells[k + 4], cells[k]) for k in range(7)]
            cells = [jnp.where(bits[2], cells[k + 2], cells[k]) for k in range(5)]
            taps.append([jnp.where(bits[3], cells[k + 1], cells[k]) for k in range(4)])
        second = stencil(taps, xw, yw)
        hess_yy, hess_xx, hess_xy = first[2], first[3], first[4]
        other_yy, other_xx, other_xy = second[2], second[3], second[4]
        lensed_yy = 1.0 - lens_ratio * hess_yy
        lensed_xx = 1.0 - lens_ratio * hess_xx
        lensed_xy = -lens_ratio * hess_xy
        deflect_ref[0, :, cols] = first[0] + second[0]
        deflect_ref[1, :, cols] = first[1] + second[1]
        jacob_ref[0, :, cols] = 1.0 - hess_yy - (other_yy * lensed_yy + other_xy * lensed_xy)
        jacob_ref[1, :, cols] = -hess_xy - (other_yy * lensed_xy + other_xy * lensed_xx)
        jacob_ref[2, :, cols] = -hess_xy - (other_xy * lensed_yy + other_xx * lensed_xy)
        jacob_ref[3, :, cols] = 1.0 - hess_xx - (other_xy * lensed_xy + other_xx * lensed_xx)
        return carry

    def send(k):
        cols = pl.ds(pl.multiple_of(1024 * k, 1024), 1024)
        return [
            pltpu.make_async_copy(ref.at[:, :, cols], hbm.at[:, :, cols], sems.at[i, k])
            for i, (ref, hbm) in enumerate(((deflect_ref, deflect_hbm), (jacob_ref, jacob_hbm)))
        ]

    def chunk(k, carry):
        for t in range(8):
            tile(8 * k + t, carry)
        for copy in send(k):
            copy.start()
        return carry

    lax.fori_loop(0, 4, chunk, 0)
    for k in range(4):
        for copy in send(k):
            copy.wait()


def vmem(shape):
    return pltpu.VMEM(shape, jnp.float32)


def call(kernel, name, args, outs, scratch, ins=None, out_space=pltpu.VMEM, grant=16 * 1024 * 1024):
    spaces = [pltpu.VMEM] * len(args) if ins is None else ins
    return pl.pallas_call(
        kernel,
        name=name,
        out_shape=outs,
        in_specs=[pl.BlockSpec(memory_space=space) for space in spaces],
        out_specs=jax.tree.map(lambda _: pl.BlockSpec(memory_space=out_space), outs),
        scratch_shapes=scratch,
        compiler_params=pltpu.CompilerParams(vmem_limit_bytes=grant),
    )(*args)


def shape(*dims):
    return jax.ShapeDtypeStruct(dims, jnp.float32)


def on_device(kappa, ray_offsets):
    tab = tables()
    spectra = call(
        rows_kernel,
        "rows",
        (kappa[0], tab["row_fwd"], tab["row_turn"]),
        shape(2048, 128),
        [
            vmem((2048, 128)),
            vmem((64, N)),
            pltpu.VMEM((256, 256), jnp.bfloat16),
            vmem((2, OUTER, 128)),
            vmem((2048, 256)),
            pltpu.SemaphoreType.DMA((14,)),
        ],
        ins=[pltpu.HBM] * 3,
        out_space=pltpu.HBM,
        grant=ROWS_GRANT,
    )
    columns = lax.all_to_all(spectra.reshape(SLABS, 32, 128), "slab", split_axis=0, concat_axis=0, tiled=True)
    strips = call(
        columns_kernel,
        "columns",
        (columns, tab["col_fwd"], tab["col_turn"], tab["wave2"], tab["col_inv"], tab["col_extra"], tab["col_back"]),
        shape(2 * SLABS, 24, 128),
        [vmem((2, 512, 256)), vmem((2, 512, 128)), pltpu.VMEM((4, 512, 384), jnp.bfloat16)],
    )
    windows = lax.all_to_all(strips, ("plane", "slab"), split_axis=0, concat_axis=0, tiled=True)
    deflection, jacobian = call(
        rays_kernel,
        "rays",
        (windows, tab["row_inv"], tab["row_turn"], ray_offsets[:, 0, 0]),
        (shape(2, 8, N), shape(4, 8, N)),
        [
            vmem((2, 8, N)),
            vmem((4, 8, N)),
            vmem((OUTER * WIN, 128)),
            vmem((OUTER * WIN, 256)),
            vmem((5, OUTER * NEAR_WIN, 128)),
            vmem((OUTER * WIN, 128)),
            vmem((OUTER * WIN, 128)),
            pltpu.SemaphoreType.DMA((2, 4)),
        ],
        out_space=pltpu.HBM,
    )
    return deflection[:, None, None], jacobian[:, None, None]


def solution(mesh):
    placed = (P("plane", "slab", None), P(None, "slab", "plane", None, None))
    return jax.shard_map(
        on_device,
        mesh=mesh,
        in_specs=placed,
        out_specs=(P(None, "slab", "plane", None, None), P(None, "slab", "plane", None, None)),
        check_vma=False,
    )
```

```python
import functools
import math

import jax
import jax.numpy as jnp
import numpy as np
from jax import lax
from jax.experimental import pallas as pl
from jax.experimental.pallas import tpu as pltpu
from jax.sharding import PartitionSpec as P

N = 4096
OUTER = 32
SLABS = 64
PATCH_ROWS = 16
NEAR_WIN = 40
WIN = 48
ROWS_GRANT = 62 * 1024 * 1024
NEAR_STEP = 4
FAR_STEP = 4
LEAD = 5
lens_ratio = 0.5
screen_modes = 4.0


def angles(left, right, length):
    return (np.outer(left, right) % length) * (2.0 * np.pi / length)


def cas_pair(left, right, length):
    a = angles(left, right, length)
    return np.cos(a) + np.sin(a), np.cos(a) - np.sin(a)


def f32(table):
    return np.asarray(table, np.float32)


def parts(table, count):
    out = []
    for _ in range(count):
        out.append(np.asarray(table, jnp.bfloat16))
        table = table - np.asarray(out[-1], np.float64)
    return out


@functools.cache
def tables():
    out = {}
    lane = np.arange(128)
    plus, minus = cas_pair(lane, lane, 128)
    both = np.concatenate([plus, minus], axis=0)
    out["row_fwd"] = np.concatenate(parts(both, 2), axis=1)
    turn = angles(np.arange(OUTER), lane, N)
    out["row_turn"] = f32(np.stack([np.cos(turn), np.sin(turn)]))
    out["row_inv"] = np.stack(parts(0.5 * np.concatenate([plus, -minus], axis=1), 3))
    sixty = np.arange(64)
    plus, minus = cas_pair(sixty, sixty, 64)
    two = np.eye(2)
    both = np.concatenate([np.kron(two, plus), np.kron(two, minus)], axis=0)
    out["col_fwd"] = np.concatenate(parts(both, 2), axis=1)
    turn = angles(sixty, np.concatenate([sixty, sixty]), N)
    out["col_turn"] = f32(np.stack([np.cos(turn), np.sin(turn)]))
    inv, extra, turns = [], [], []
    for p in range(2):
        rows = 32 * p - LEAD + np.arange(WIN)
        plus, minus = cas_pair(sixty, rows, 64)
        table = 0.5 * np.stack([np.kron(two, plus), -np.kron(two, minus)], axis=1)
        turn = angles(sixty, np.concatenate([rows, rows]), N)
        inv.append(np.pad(table, ((0, 0), (0, 0), (0, 32))).reshape(128, 256))
        for k in range(3):
            own = slice(32 * k, 32 * k + 32)
            extra.append(np.pad(table[:, :, own], ((0, 0), (0, 0), (96, 0))).reshape(128, 256))
            full = np.concatenate([turn, turn[:, own]], axis=1)
            turns.append(np.stack([np.cos(full), np.sin(full)]))
    out["col_inv"] = np.stack([np.stack(parts(table, 3)) for table in inv])
    out["col_extra"] = np.stack([np.stack(parts(table, 3)) for table in extra]).reshape(2, 3, 3, 128, 256)
    out["col_back"] = f32(np.stack(turns).reshape(2, 3, 2, 64, 128))
    ids = np.arange(64)[:, None] + 64 * np.concatenate([sixty, sixty])[None, :]
    wave = 2.0 * np.pi / N * np.minimum(ids, N - ids)
    out["wave2"] = f32(wave**2)
    return out


def cmul(re, im, c, s):
    if abs(s) < 1e-12 and abs(c - 1.0) < 1e-12:
        return re, im
    if abs(c) < 1e-12 and abs(s - 1.0) < 1e-12:
        return (None if im is None else -im), re
    if im is None:
        return re * c, re * s
    if re is None:
        return im * (-s), im * c
    if abs(c - s) < 1e-12:
        return (re - im) * c, (re + im) * c
    if abs(c + s) < 1e-12:
        return (re + im) * c, (im - re) * c
    return re * c - im * s, re * s + im * c


def add(a, b):
    return b if a is None else a if b is None else a + b


def sub(a, b):
    return a if b is None else -b if a is None else a - b


def neg(a):
    return None if a is None else -a


def real_to_half(xs):
    n = len(xs)
    if n == 2:
        return [(xs[0] + xs[1], None), (xs[0] - xs[1], None)]
    even, odd = real_to_half(xs[0::2]), real_to_half(xs[1::2])
    half = n // 2
    out = [None] * (half + 1)
    for k in range(half // 2 + 1):
        c, s = math.cos(2 * math.pi * k / n), math.sin(2 * math.pi * k / n)
        tr, ti = cmul(*odd[k], c, s)
        er, ei = even[k]
        out[k] = (add(er, tr), add(ei, ti))
        if half - k != k:
            out[half - k] = (sub(er, tr), sub(ti, ei))
    return out


def half_to_real(xs):
    half = len(xs) - 1
    n = 2 * half
    if n == 2:
        return [xs[0][0] + xs[1][0], xs[0][0] - xs[1][0]]
    even, odd = [], []
    for k in range(half // 2 + 1):
        ar, ai = xs[k]
        br, bi = xs[half - k]
        if k == half - k:
            even.append((ar + ar, None))
            odd.append((-(ai + ai), None))
            continue
        even.append((add(ar, br), sub(ai, bi)))
        c, s = math.cos(2 * math.pi * k / n), math.sin(2 * math.pi * k / n)
        odd.append(cmul(sub(ar, br), add(ai, bi), c, s))
    evens, odds = half_to_real(even), half_to_real(odd)
    return [v for pair in zip(evens, odds) for v in pair]


def row8(ref, *index):
    return jnp.broadcast_to(ref[index], (8, 128))


def turned(re, im, c, s):
    if im is None:
        return re * c, re * s
    return re * c - im * s, re * s + im * c


def forward_outer(xs, turn_ref, store):
    n = len(xs)
    half = real_to_half(xs)
    for m in range(n):
        re, im = half[m] if m <= n // 2 else (half[n - m][0], neg(half[n - m][1]))
        store(m, *turned(re, im, row8(turn_ref, 0, slice(m, m + 1)), row8(turn_ref, 1, slice(m, m + 1))))


def inverse_outer(load, n, turn_ref, *lead):
    def value(m):
        re, im = load(m)
        return turned(re, im, row8(turn_ref, *lead, 0, slice(m, m + 1)), row8(turn_ref, *lead, 1, slice(m, m + 1)))

    spectrum = []
    for m in range(n // 2 + 1):
        re, im = value(m)
        if m in (0, n // 2):
            spectrum.append((re + re, None))
        else:
            ro, io = value(n - m)
            spectrum.append((re + ro, im - io))
    return half_to_real(spectrum)


def split(x, count):
    out = []
    for i in range(count):
        out.append(x.astype(jnp.bfloat16))
        if i + 1 < count:
            x = x - out[-1].astype(jnp.float32)
    return out


def left_of(pieces):
    a, b, c = (pieces[:, 128 * i : 128 * i + 128] for i in range(3))
    return [a, b, a, b, a, c]


def right_of(w):
    return [w[0], w[0], w[1], w[1], w[2], w[0]]


def fine_dot(x, w):
    left = jnp.concatenate(left_of(jnp.concatenate(split(x, 3), axis=1)), axis=1)
    return jnp.dot(left, jnp.concatenate(right_of(w), axis=0), preferred_element_type=jnp.float32)


def coarse_dot(x, w):
    left = jnp.concatenate(split(x, 2), axis=1)
    both = jnp.dot(left, jnp.concatenate([w, w], axis=0), preferred_element_type=jnp.float32)
    return both[:, :128] + both[:, 128:]


def rows_kernel(kappa_hbm, weight_hbm, turn_hbm, out_hbm, out_ref, kappa_ref, weight_ref, turn_ref, mid, sems):
    def fetch(g):
        rows = pl.ds(8 * g, 8)
        return pltpu.make_async_copy(kappa_hbm.at[rows, :], kappa_ref.at[rows, :], sems.at[g])

    def send(i):
        rows = pl.ds(512 * i, 512)
        return pltpu.make_async_copy(out_ref.at[rows, :], out_hbm.at[rows, :], sems.at[10 + i])

    turn_copy = pltpu.make_async_copy(turn_hbm, turn_ref, sems.at[8])
    weight_copy = pltpu.make_async_copy(weight_hbm, weight_ref, sems.at[9])
    turn_copy.start()
    for g in range(8):
        fetch(g).start()
    weight_copy.start()
    turn_copy.wait()
    for g in range(8):
        fetch(g).wait()
        xs = [kappa_ref[8 * g : 8 * g + 8, 128 * j : 128 * j + 128] for j in range(OUTER)]

        def store(m, re, im):
            mid[64 * m + 8 * g : 64 * m + 8 * g + 8, 0:128] = re
            mid[64 * m + 8 * g : 64 * m + 8 * g + 8, 128:256] = im

        forward_outer(xs, turn_ref, store)
    weight_copy.wait()
    for i in range(4):
        found = coarse_dot(mid[512 * i : 512 * i + 512, :], weight_ref[...])
        for k in range(4):
            out_ref[512 * i + 128 * k : 512 * i + 128 * k + 128, :] = jnp.transpose(found[128 * k : 128 * k + 128])
        send(i).start()
    for i in range(4):
        send(i).wait()


def columns_kernel(in_ref, fwd_ref, turn_ref, wave_ref, inv_ref, extra_ref, back_ref, out_ref, mids, specs, pieces):
    owner = lax.axis_index("slab")
    base = 2 * lax.div(owner, 4) + 1024 * lax.rem(owner, 4)
    lane = lax.broadcasted_iota(jnp.int32, (8, 128), 1)
    sub8 = lax.broadcasted_iota(jnp.int32, (8, 128), 0)
    screen = (2.0 * math.pi * screen_modes / N) ** 2

    def forward(g, mid, spec):
        rows = pl.ds(pl.multiple_of(8 * g, 8), 8)
        xs = [in_ref[s, rows, :] for s in range(SLABS)]

        def store(m, re, im):
            mid[8 * m : 8 * m + 8, 0:128] = re
            mid[8 * m : 8 * m + 8, 128:256] = im

        forward_outer(xs, turn_ref, store)
        spec[...] = coarse_dot(mid[...], fwd_ref[...])
        ids = base + jnp.where(lane >= 64, 1, 0) + 32 * (8 * g + sub8)
        wave = (2.0 * math.pi / N) * jnp.minimum(ids, N - ids).astype(jnp.float32)
        mine = wave * wave + screen
        for m in range(SLABS):
            factor = -2.0 / ((mine + row8(wave_ref, slice(m, m + 1))) * float(N * N))
            if m == 0:
                factor = jnp.where((ids == 0) & (lane == 0), 0.0, factor)
            spec[8 * m : 8 * m + 8, :] = spec[8 * m : 8 * m + 8, :] * factor
        for i, piece in enumerate(split(spec[...], 3)):
            pieces[g, :, 128 * i : 128 * i + 128] = piece

    def forward_pair(i, carry):
        forward(2 * i, mids.at[0], specs.at[0])
        forward(2 * i + 1, mids.at[1], specs.at[1])
        return carry

    lax.fori_loop(0, 2, forward_pair, 0, unroll=2)

    def backward(k, carry):
        for p in range(2):
            mid = mids.at[p]
            left = left_of(pieces[k]) + left_of(pieces[3])
            right = right_of(inv_ref[p]) + right_of(extra_ref[p, k])
            mid[...] = jnp.dot(
                jnp.concatenate(left, axis=1), jnp.concatenate(right, axis=0), preferred_element_type=jnp.float32
            )
            values = inverse_outer(
                lambda m: (mid[8 * m : 8 * m + 8, 0:128], mid[8 * m : 8 * m + 8, 128:256]), SLABS, back_ref, p, k
            )
            rows = pl.ds(pl.multiple_of(8 * k, 8), 8)
            for s in range(SLABS):
                out_ref[p * SLABS + s, rows, :] = values[s]
        return carry

    lax.fori_loop(0, 3, backward, 0, unroll=3)


def spline_weights(f):
    e = 1.0 - f
    f2, e2 = f * f, e * e
    f3, e3 = f2 * f, e2 * e
    sixth, third = 1.0 / 6.0, 2.0 / 3.0
    value = [e3 * sixth, third - f2 + 0.5 * f3, third - e2 + 0.5 * e3, f3 * sixth]
    slope = [-0.5 * e2, 1.5 * f2 - 2.0 * f, 2.0 * e - 1.5 * e2, 0.5 * f2]
    curve = [e, 3.0 * f - 2.0, 1.0 - 3.0 * f, f]
    return value, slope, curve


def dot4(ws, vs):
    return (ws[0] * vs[0] + ws[1] * vs[1]) + (ws[2] * vs[2] + ws[3] * vs[3])


def stencil(taps, xw, yw):
    rows = list(zip(*taps))
    flat = [dot4(xw[0], row) for row in rows]
    slope = [dot4(xw[1], row) for row in rows]
    curve = [dot4(xw[2], row) for row in rows]
    return across_rows(flat, slope, curve, yw)


def across_rows(flat, slope, curve, yw):
    return dot4(yw[1], flat), dot4(yw[0], slope), dot4(yw[2], flat), dot4(yw[0], curve), dot4(yw[1], slope)


def kept(weights, cells, count):
    inside = [(cell >= 0) & (cell < count) for cell in cells]
    return [[jnp.where(inside[c], w[c], 0.0) for c in range(len(cells))] for w in weights]


def lane_gather(values, spots):
    dims = lax.GatherDimensionNumbers(
        offset_dims=(), collapsed_slice_dims=(1,), start_index_map=(1,),
        operand_batching_dims=(0,), start_indices_batching_dims=(0,),
    )
    return lax.gather(
        values, spots[..., None], dims, (1, 1), mode=lax.GatherScatterMode.PROMISE_IN_BOUNDS
    )


def rays_kernel(
    in_ref, inv_ref, turn_ref, off_ref, deflect_hbm, jacob_hbm, deflect_ref, jacob_ref, flat, mid, near, even, odd, first, pos, halves, sems
):
    lane = lax.broadcasted_iota(jnp.int32, (8, 128), 1)

    for q, win in enumerate((NEAR_WIN, WIN)):
        def unpack(i, carry):
            rows = []
            for d in range(4):
                got = [in_ref[q * SLABS + 4 * i + d, 8 * k : 8 * k + 8, :] for k in range(3)]
                moved = [pltpu.roll(got[k], 32 + 32 * k, 1) for k in range(3)]
                rows += got
                rows.append(jnp.where(lane < 32, moved[0], jnp.where(lane < 64, moved[1], moved[2])))
            block = jnp.transpose(jnp.concatenate(rows, axis=0))
            for h in range(2):
                spot = pl.ds(pl.multiple_of(win * (2 * i + h), 8), win)
                flat[spot, :] = block[WIN * h : WIN * h + win]
            return carry

        lax.fori_loop(0, 16, unpack, 0, unroll=8)
        for half in (slice(0, 16 * win), slice(16 * win, 32 * win)):
            mid[half, :] = fine_dot(flat[half, :], inv_ref[...])

        def finish(g, carry):
            def load(m):
                spot = pl.ds(pl.multiple_of(win * m + 8 * g, 8), 8)
                return mid[spot, 0:128], mid[spot, 128:256]

            values = inverse_outer(load, OUTER, turn_ref)

            def spot(t):
                return pl.ds(pl.multiple_of(win * t + 8 * g, 8), 8)

            if q == 0:
                for t in range(OUTER):
                    near[2, spot(t), :] = values[t]
                for d in (-2, -1, 1, 2):
                    moved = [pltpu.roll(v, (-d) % 128, 1) for v in values]
                    for t in range(OUTER):
                        if d < 0:
                            v = jnp.where(lane < -d, moved[t - 1], moved[t])
                        else:
                            v = jnp.where(lane < 128 - d, moved[t], moved[(t + 1) % OUTER])
                        near[2 + d, spot(t), :] = v
            else:
                moved = [pltpu.roll(v, 32, 1) for v in values]
                for t in range(OUTER):
                    even[spot(t), :] = jnp.where(lane < 32, moved[t - 1], moved[t])
                moved = [pltpu.roll(v, 96, 1) for v in values]
                for t in range(OUTER):
                    odd[spot(t), :] = jnp.where(lane < 96, moved[t], moved[(t + 1) % OUTER])
            return carry

        lax.fori_loop(0, win // 8, finish, 0, unroll=5 if q == 0 else 3)

    low_half = lane < 64

    def spot8(t):
        return pl.ds(pl.multiple_of(8 * t, 8), 8)

    def near_tile(t):
        cols = pl.ds(pl.multiple_of(128 * t, 128), 128)
        off_y = off_ref[0, :, cols]
        off_x = off_ref[1, :, cols]
        rel_y = 4.0 * off_y
        low_y = jnp.minimum(jnp.floor(rel_y), 1.0)
        left = off_x < 0.0
        frac_x = jnp.where(left, off_x + 1.0, off_x)
        bits = [low_y >= 0.0, (low_y == -1.0) | (low_y == 1.0)]
        taps = []
        for c in range(4):
            cells = []
            for j in range(4, 11):
                rows = pl.ds(NEAR_WIN * t + j, 8, stride=4)
                cells.append(jnp.where(left, near[c, rows, :], near[c + 1, rows, :]))
            cells = [jnp.where(bits[0], cells[k + 2], cells[k]) for k in range(5)]
            taps.append([jnp.where(bits[1], cells[k + 1], cells[k]) for k in range(4)])
        found = stencil(taps, spline_weights(frac_x), spline_weights(rel_y - low_y))
        pos_y = (7.0 + rel_y) - lens_ratio * found[0]
        start = (32 + lax.rem(lane, 64)).astype(jnp.float32)
        pos_x = (start + off_x) - lens_ratio * found[1]
        for i in range(5):
            first[i, spot8(t), :] = found[i]
        pos[0, spot8(t), :] = pos_x
        pos[1, spot8(t), :] = pos_y
        pos[2, spot8(t), :] = pltpu.roll(pos_x, 64, 1)
        pos[3, spot8(t), :] = pltpu.roll(pos_y, 64, 1)

    def far_tile(t):
        for side, (source, mask) in enumerate(((even, low_half), (odd, ~low_half))):
            block_x = jnp.where(mask, pos[0, spot8(t), :], pos[2, spot8(t), :])
            block_y = jnp.where(mask, pos[1, spot8(t), :], pos[3, spot8(t), :])
            low_x = jnp.floor(block_x)
            cell_x = jnp.clip(low_x, -8.0, 136.0).astype(jnp.int32) - jnp.where(low_half, 1, 0)
            cell_y = jnp.clip(jnp.floor(block_y), -8.0, 32.0).astype(jnp.int32) - 1
            weights = spline_weights(block_x - low_x)
            weights = [[jnp.where(low_half, w[2 * c], w[2 * c + 1]) for c in range(2)] for w in weights]
            spots = [cell_x, cell_x + 2]
            xw = kept(weights, spots, 128)
            bits = [(cell_y & b) != 0 for b in (8, 4, 2, 1)]
            taps = []
            for c in range(2):
                spot = jnp.clip(spots[c], 0, 127)
                cells = []
                for j in range(PATCH_ROWS):
                    cells.append(lane_gather(source[pl.ds(WIN * t + j, 8, stride=4), :], spot))
                cells = [jnp.where(bits[0], cells[(k + 8) % 16], cells[k]) for k in range(11)]
                cells = [jnp.where(bits[1], cells[k + 4], cells[k]) for k in range(7)]
                cells = [jnp.where(bits[2], cells[k + 2], cells[k]) for k in range(5)]
                taps.append([jnp.where(bits[3], cells[k + 1], cells[k]) for k in range(4)])
            for i, w in enumerate(xw):
                for r in range(4):
                    halves[side, 4 * i + r, spot8(t), :] = w[0] * taps[0][r] + w[1] * taps[1][r]

    def last_tile(t):
        cols = pl.ds(pl.multiple_of(128 * t, 128), 128)
        across = []
        for i in range(12):
            e, o = halves[0, i, spot8(t), :], halves[1, i, spot8(t), :]
            across.append(jnp.where(low_half, e, o) + pltpu.roll(jnp.where(low_half, o, e), 64, 1))
        pos_y = pos[1, spot8(t), :]
        low_y = jnp.floor(pos_y)
        cell_y = jnp.clip(low_y, -8.0, 32.0).astype(jnp.int32) - 1
        yw = kept(spline_weights(pos_y - low_y), [cell_y + c for c in range(4)], PATCH_ROWS)
        second = across_rows(across[0:4], across[4:8], across[8:12], yw)
        slope_y, slope_x, hess_yy, hess_xx, hess_xy = [first[i, spot8(t), :] for i in range(5)]
        other_yy, other_xx, other_xy = second[2], second[3], second[4]
        lensed_yy = 1.0 - lens_ratio * hess_yy
        lensed_xx = 1.0 - lens_ratio * hess_xx
        lensed_xy = -lens_ratio * hess_xy
        deflect_ref[0, :, cols] = slope_y + second[0]
        deflect_ref[1, :, cols] = slope_x + second[1]
        jacob_ref[0, :, cols] = 1.0 - hess_yy - (other_yy * lensed_yy + other_xy * lensed_xy)
        jacob_ref[1, :, cols] = -hess_xy - (other_yy * lensed_xy + other_xy * lensed_xx)
        jacob_ref[2, :, cols] = -hess_xy - (other_xy * lensed_yy + other_xx * lensed_xy)
        jacob_ref[3, :, cols] = 1.0 - hess_xx - (other_xy * lensed_xy + other_xx * lensed_xx)

    def several(step, count):
        def body(i, carry):
            for k in range(count):
                step(count * i + k)
            return carry

        return body

    def send(k):
        cols = pl.ds(pl.multiple_of(1024 * k, 1024), 1024)
        return [
            pltpu.make_async_copy(ref.at[:, :, cols], hbm.at[:, :, cols], sems.at[i, k])
            for i, (ref, hbm) in enumerate(((deflect_ref, deflect_hbm), (jacob_ref, jacob_hbm)))
        ]

    def body(i, carry):
        for k in range(FAR_STEP):
            last_tile(FAR_STEP * i - FAR_STEP + k)
            far_tile(FAR_STEP * i + k)
            near_tile(FAR_STEP * i + FAR_STEP + k)

        @pl.when(lax.rem(i, 2) == 0)
        def _():
            for copy in send(lax.div(i, 2) - 1):
                copy.start()

        return carry

    for k in range(FAR_STEP):
        near_tile(k)
    for k in range(FAR_STEP):
        far_tile(k)
        near_tile(FAR_STEP + k)
    lax.fori_loop(1, OUTER // FAR_STEP - 1, body, 0)
    for k in range(FAR_STEP):
        last_tile(OUTER - 2 * FAR_STEP + k)
        far_tile(OUTER - FAR_STEP + k)
    for k in range(FAR_STEP):
        last_tile(OUTER - FAR_STEP + k)
    for copy in send(3):
        copy.start()
    for k in range(4):
        for copy in send(k):
            copy.wait()


def vmem(shape):
    return pltpu.VMEM(shape, jnp.float32)


def call(kernel, name, args, outs, scratch, ins=None, out_space=pltpu.VMEM, grant=16 * 1024 * 1024):
    spaces = [pltpu.VMEM] * len(args) if ins is None else ins
    return pl.pallas_call(
        kernel,
        name=name,
        out_shape=outs,
        in_specs=[pl.BlockSpec(memory_space=space) for space in spaces],
        out_specs=jax.tree.map(lambda _: pl.BlockSpec(memory_space=out_space), outs),
        scratch_shapes=scratch,
        compiler_params=pltpu.CompilerParams(vmem_limit_bytes=grant),
    )(*args)


def shape(*dims):
    return jax.ShapeDtypeStruct(dims, jnp.float32)


def on_device(kappa, ray_offsets):
    tab = tables()
    spectra = call(
        rows_kernel,
        "rows",
        (kappa[0], tab["row_fwd"], tab["row_turn"]),
        shape(2048, 128),
        [
            vmem((2048, 128)),
            vmem((64, N)),
            pltpu.VMEM((256, 256), jnp.bfloat16),
            vmem((2, OUTER, 128)),
            vmem((2048, 256)),
            pltpu.SemaphoreType.DMA((14,)),
        ],
        ins=[pltpu.HBM] * 3,
        out_space=pltpu.HBM,
        grant=ROWS_GRANT,
    )
    columns = lax.all_to_all(spectra.reshape(SLABS, 32, 128), "slab", split_axis=0, concat_axis=0, tiled=True)
    strips = call(
        columns_kernel,
        "columns",
        (columns, tab["col_fwd"], tab["col_turn"], tab["wave2"], tab["col_inv"], tab["col_extra"], tab["col_back"]),
        shape(2 * SLABS, 24, 128),
        [vmem((2, 512, 256)), vmem((2, 512, 128)), pltpu.VMEM((4, 512, 384), jnp.bfloat16)],
    )
    windows = lax.all_to_all(strips, ("plane", "slab"), split_axis=0, concat_axis=0, tiled=True)
    deflection, jacobian = call(
        rays_kernel,
        "rays",
        (windows, tab["row_inv"], tab["row_turn"], ray_offsets[:, 0, 0]),
        (shape(2, 8, N), shape(4, 8, N)),
        [
            vmem((2, 8, N)),
            vmem((4, 8, N)),
            vmem((OUTER * WIN, 128)),
            vmem((OUTER * WIN, 256)),
            vmem((5, OUTER * NEAR_WIN, 128)),
            vmem((OUTER * WIN, 128)),
            vmem((OUTER * WIN, 128)),
            vmem((5, 8 * OUTER, 128)),
            vmem((4, 8 * OUTER, 128)),
            vmem((2, 12, 8 * OUTER, 128)),
            pltpu.SemaphoreType.DMA((2, 4)),
        ],
        grant=20 * 1024 * 1024,
        out_space=pltpu.HBM,
    )
    return deflection[:, None, None], jacobian[:, None, None]


def solution(mesh):
    placed = (P("plane", "slab", None), P(None, "slab", "plane", None, None))
    return jax.shard_map(
        on_device,
        mesh=mesh,
        in_specs=placed,
        out_specs=(P(None, "slab", "plane", None, None), P(None, "slab", "plane", None, None)),
        check_vma=False,
    )
```

```python
import functools
import math

import jax
import jax.numpy as jnp
import numpy as np
from jax import lax
from jax.experimental import pallas as pl
from jax.experimental.pallas import tpu as pltpu
from jax.sharding import PartitionSpec as P

N = 4096
OUTER = 32
SLABS = 64
PATCH_ROWS = 16
NEAR_WIN = 40
WIN = 48
ROWS_GRANT = 62 * 1024 * 1024
NEAR_STEP = 4
FAR_STEP = 4
LEAD = 5
lens_ratio = 0.5
screen_modes = 4.0


def angles(left, right, length):
    return (np.outer(left, right) % length) * (2.0 * np.pi / length)


def cas_pair(left, right, length):
    a = angles(left, right, length)
    return np.cos(a) + np.sin(a), np.cos(a) - np.sin(a)


def f32(table):
    return np.asarray(table, np.float32)


def parts(table, count):
    out = []
    for _ in range(count):
        out.append(np.asarray(table, jnp.bfloat16))
        table = table - np.asarray(out[-1], np.float64)
    return out


@functools.cache
def tables():
    out = {}
    lane = np.arange(128)
    plus, minus = cas_pair(lane, lane, 128)
    both = np.concatenate([plus, minus], axis=0)
    out["row_fwd"] = np.concatenate(parts(both, 2), axis=1)
    turn = angles(np.arange(OUTER), lane, N)
    out["row_turn"] = f32(np.stack([np.cos(turn), np.sin(turn)]))
    out["row_inv"] = np.stack(parts(0.5 * np.concatenate([plus, -minus], axis=1), 3))
    sixty = np.arange(64)
    plus, minus = cas_pair(sixty, sixty, 64)
    two = np.eye(2)
    both = np.concatenate([np.kron(two, plus), np.kron(two, minus)], axis=0)
    out["col_fwd"] = np.concatenate(parts(both, 2), axis=1)
    turn = angles(sixty, np.concatenate([sixty, sixty]), N)
    out["col_turn"] = f32(np.stack([np.cos(turn), np.sin(turn)]))
    inv, turns = [], []
    for p in range(2):
        rows = 32 * p - LEAD + np.arange(WIN)
        plus, minus = cas_pair(sixty, rows, 64)
        table = 0.5 * np.stack([np.kron(two, plus), -np.kron(two, minus)], axis=1)
        turn = angles(sixty, np.concatenate([rows, rows]), N)
        for k in range(3):
            own = slice(32 * k, 32 * k + 32)
            inv.append(np.concatenate([table, table[:, :, own]], axis=2).reshape(128, 256))
            full = np.concatenate([turn, turn[:, own]], axis=1)
            turns.append(np.stack([np.cos(full), np.sin(full)]))
    out["col_inv"] = np.stack([np.stack(parts(table, 3)) for table in inv]).reshape(2, 3, 3, 128, 256)
    out["col_back"] = f32(np.stack(turns).reshape(2, 3, 2, 64, 128))
    ids = np.arange(64)[:, None] + 64 * np.concatenate([sixty, sixty])[None, :]
    wave = 2.0 * np.pi / N * np.minimum(ids, N - ids)
    out["wave2"] = f32(wave**2)
    return out


def cmul(re, im, c, s):
    if abs(s) < 1e-12 and abs(c - 1.0) < 1e-12:
        return re, im
    if abs(c) < 1e-12 and abs(s - 1.0) < 1e-12:
        return (None if im is None else -im), re
    if im is None:
        return re * c, re * s
    if re is None:
        return im * (-s), im * c
    if abs(c - s) < 1e-12:
        return (re - im) * c, (re + im) * c
    if abs(c + s) < 1e-12:
        return (re + im) * c, (im - re) * c
    return re * c - im * s, re * s + im * c


def add(a, b):
    return b if a is None else a if b is None else a + b


def sub(a, b):
    return a if b is None else -b if a is None else a - b


def neg(a):
    return None if a is None else -a


def real_to_half(xs):
    n = len(xs)
    if n == 2:
        return [(xs[0] + xs[1], None), (xs[0] - xs[1], None)]
    even, odd = real_to_half(xs[0::2]), real_to_half(xs[1::2])
    half = n // 2
    out = [None] * (half + 1)
    for k in range(half // 2 + 1):
        c, s = math.cos(2 * math.pi * k / n), math.sin(2 * math.pi * k / n)
        tr, ti = cmul(*odd[k], c, s)
        er, ei = even[k]
        out[k] = (add(er, tr), add(ei, ti))
        if half - k != k:
            out[half - k] = (sub(er, tr), sub(ti, ei))
    return out


def half_to_real(xs):
    half = len(xs) - 1
    n = 2 * half
    if n == 2:
        return [xs[0][0] + xs[1][0], xs[0][0] - xs[1][0]]
    even, odd = [], []
    for k in range(half // 2 + 1):
        ar, ai = xs[k]
        br, bi = xs[half - k]
        if k == half - k:
            even.append((ar + ar, None))
            odd.append((-(ai + ai), None))
            continue
        even.append((add(ar, br), sub(ai, bi)))
        c, s = math.cos(2 * math.pi * k / n), math.sin(2 * math.pi * k / n)
        odd.append(cmul(sub(ar, br), add(ai, bi), c, s))
    evens, odds = half_to_real(even), half_to_real(odd)
    return [v for pair in zip(evens, odds) for v in pair]


def row8(ref, *index):
    return jnp.broadcast_to(ref[index], (8, 128))


def turned(re, im, c, s):
    if im is None:
        return re * c, re * s
    return re * c - im * s, re * s + im * c


def forward_outer(xs, turn_ref, store):
    n = len(xs)
    half = real_to_half(xs)
    for m in range(n):
        re, im = half[m] if m <= n // 2 else (half[n - m][0], neg(half[n - m][1]))
        store(m, *turned(re, im, row8(turn_ref, 0, slice(m, m + 1)), row8(turn_ref, 1, slice(m, m + 1))))


def inverse_outer(load, n, turn_ref, *lead):
    def value(m):
        re, im = load(m)
        return turned(re, im, row8(turn_ref, *lead, 0, slice(m, m + 1)), row8(turn_ref, *lead, 1, slice(m, m + 1)))

    spectrum = []
    for m in range(n // 2 + 1):
        re, im = value(m)
        if m in (0, n // 2):
            spectrum.append((re + re, None))
        else:
            ro, io = value(n - m)
            spectrum.append((re + ro, im - io))
    return half_to_real(spectrum)


def split(x, count):
    out = []
    for i in range(count):
        out.append(x.astype(jnp.bfloat16))
        if i + 1 < count:
            x = x - out[-1].astype(jnp.float32)
    return out


def left_of(pieces):
    a, b, c = (pieces[:, 128 * i : 128 * i + 128] for i in range(3))
    return [a, b, a, b, a, c]


def right_of(w):
    return [w[0], w[0], w[1], w[1], w[2], w[0]]


def fine_dot(x, w):
    left = jnp.concatenate(left_of(jnp.concatenate(split(x, 3), axis=1)), axis=1)
    return jnp.dot(left, jnp.concatenate(right_of(w), axis=0), preferred_element_type=jnp.float32)


def coarse_dot(x, w):
    left = jnp.concatenate(split(x, 2), axis=1)
    both = jnp.dot(left, jnp.concatenate([w, w], axis=0), preferred_element_type=jnp.float32)
    return both[:, :128] + both[:, 128:]


def rows_kernel(kappa_hbm, weight_hbm, turn_hbm, out_hbm, out_ref, kappa_ref, weight_ref, turn_ref, mid, sems):
    def fetch(g):
        rows = pl.ds(8 * g, 8)
        return pltpu.make_async_copy(kappa_hbm.at[rows, :], kappa_ref.at[rows, :], sems.at[g])

    def send(i):
        rows = pl.ds(512 * i, 512)
        return pltpu.make_async_copy(out_ref.at[rows, :], out_hbm.at[rows, :], sems.at[10 + i])

    turn_copy = pltpu.make_async_copy(turn_hbm, turn_ref, sems.at[8])
    weight_copy = pltpu.make_async_copy(weight_hbm, weight_ref, sems.at[9])
    turn_copy.start()
    for g in range(8):
        fetch(g).start()
    weight_copy.start()
    turn_copy.wait()
    for g in range(8):
        fetch(g).wait()
        xs = [kappa_ref[8 * g : 8 * g + 8, 128 * j : 128 * j + 128] for j in range(OUTER)]

        def store(m, re, im):
            mid[64 * m + 8 * g : 64 * m + 8 * g + 8, 0:128] = re
            mid[64 * m + 8 * g : 64 * m + 8 * g + 8, 128:256] = im

        forward_outer(xs, turn_ref, store)
    weight_copy.wait()
    for i in range(4):
        found = coarse_dot(mid[512 * i : 512 * i + 512, :], weight_ref[...])
        for k in range(4):
            out_ref[512 * i + 128 * k : 512 * i + 128 * k + 128, :] = jnp.transpose(found[128 * k : 128 * k + 128])
        send(i).start()
    for i in range(4):
        send(i).wait()


def columns_kernel(in_ref, fwd_ref, turn_ref, wave_ref, inv_ref, back_ref, out_ref, mids, specs, pieces):
    owner = lax.axis_index("slab")
    base = 2 * lax.div(owner, 4) + 1024 * lax.rem(owner, 4)
    lane = lax.broadcasted_iota(jnp.int32, (8, 128), 1)
    sub8 = lax.broadcasted_iota(jnp.int32, (8, 128), 0)
    screen = (2.0 * math.pi * screen_modes / N) ** 2

    def forward(g, mid, spec):
        rows = pl.ds(pl.multiple_of(8 * g, 8), 8)
        xs = [in_ref[s, rows, :] for s in range(SLABS)]

        def store(m, re, im):
            mid[8 * m : 8 * m + 8, 0:128] = re
            mid[8 * m : 8 * m + 8, 128:256] = im

        forward_outer(xs, turn_ref, store)
        spec[...] = coarse_dot(mid[...], fwd_ref[...])
        ids = base + jnp.where(lane >= 64, 1, 0) + 32 * (8 * g + sub8)
        wave = (2.0 * math.pi / N) * jnp.minimum(ids, N - ids).astype(jnp.float32)
        mine = wave * wave + screen
        for m in range(SLABS):
            factor = -2.0 / ((mine + row8(wave_ref, slice(m, m + 1))) * float(N * N))
            if m == 0:
                factor = jnp.where((ids == 0) & (lane == 0), 0.0, factor)
            spec[8 * m : 8 * m + 8, :] = spec[8 * m : 8 * m + 8, :] * factor
        for i, piece in enumerate(split(spec[...], 3)):
            pieces[g, :, 128 * i : 128 * i + 128] = piece

    def forward_pair(i, carry):
        forward(2 * i, mids.at[0], specs.at[0])
        forward(2 * i + 1, mids.at[1], specs.at[1])
        return carry

    lax.fori_loop(0, 2, forward_pair, 0, unroll=2)

    def backward(k, carry):
        slot = lax.rem(lax.broadcasted_iota(jnp.int32, (128, 256), 1), 128) // 32
        given = jnp.where(slot == k, 1.0, 0.0)
        taken, given = (1.0 - given).astype(jnp.bfloat16), given.astype(jnp.bfloat16)
        for p in range(2):
            mid = mids.at[p]
            left = left_of(pieces[k]) + left_of(pieces[3])
            right = right_of([inv_ref[p, k, i] * taken for i in range(3)])
            right += right_of([inv_ref[p, k, i] * given for i in range(3)])
            mid[...] = jnp.dot(
                jnp.concatenate(left, axis=1), jnp.concatenate(right, axis=0), preferred_element_type=jnp.float32
            )
            values = inverse_outer(
                lambda m: (mid[8 * m : 8 * m + 8, 0:128], mid[8 * m : 8 * m + 8, 128:256]), SLABS, back_ref, p, k
            )
            rows = pl.ds(pl.multiple_of(8 * k, 8), 8)
            for s in range(SLABS):
                out_ref[p * SLABS + s, rows, :] = values[s]
        return carry

    lax.fori_loop(0, 3, backward, 0, unroll=3)


def spline_weights(f):
    e = 1.0 - f
    f2, e2 = f * f, e * e
    f3, e3 = f2 * f, e2 * e
    sixth, third = 1.0 / 6.0, 2.0 / 3.0
    value = [e3 * sixth, third - f2 + 0.5 * f3, third - e2 + 0.5 * e3, f3 * sixth]
    slope = [-0.5 * e2, 1.5 * f2 - 2.0 * f, 2.0 * e - 1.5 * e2, 0.5 * f2]
    curve = [e, 3.0 * f - 2.0, 1.0 - 3.0 * f, f]
    return value, slope, curve


def dot4(ws, vs):
    return (ws[0] * vs[0] + ws[1] * vs[1]) + (ws[2] * vs[2] + ws[3] * vs[3])


def stencil(taps, xw, yw):
    rows = list(zip(*taps))
    flat = [dot4(xw[0], row) for row in rows]
    slope = [dot4(xw[1], row) for row in rows]
    curve = [dot4(xw[2], row) for row in rows]
    return across_rows(flat, slope, curve, yw)


def across_rows(flat, slope, curve, yw):
    return dot4(yw[1], flat), dot4(yw[0], slope), dot4(yw[2], flat), dot4(yw[0], curve), dot4(yw[1], slope)


def kept(weights, cells, count):
    inside = [(cell >= 0) & (cell < count) for cell in cells]
    return [[jnp.where(inside[c], w[c], 0.0) for c in range(len(cells))] for w in weights]


def lane_gather(values, spots):
    dims = lax.GatherDimensionNumbers(
        offset_dims=(), collapsed_slice_dims=(1,), start_index_map=(1,),
        operand_batching_dims=(0,), start_indices_batching_dims=(0,),
    )
    return lax.gather(
        values, spots[..., None], dims, (1, 1), mode=lax.GatherScatterMode.PROMISE_IN_BOUNDS
    )


def rays_kernel(
    in_ref, inv_ref, turn_ref, off_ref, deflect_hbm, jacob_hbm, deflect_ref, jacob_ref, flat, mid, near, even, odd, first, pos, halves, sems
):
    lane = lax.broadcasted_iota(jnp.int32, (8, 128), 1)

    row_group = lax.rem(lax.broadcasted_iota(jnp.int32, (32, 128), 1), 32) // 8

    for q, win in enumerate((NEAR_WIN, WIN)):
        def unpack(i, carry):
            rows = []
            for d in range(4):
                got = [in_ref[q * SLABS + 4 * i + d, 8 * k : 8 * k + 8, :] for k in range(3)]
                rows += got
                rows.append(jnp.where(lane < 32, got[0], jnp.where(lane < 64, got[1], got[2])))
            block = jnp.transpose(jnp.concatenate(rows, axis=0))
            block = jnp.concatenate(
                [jnp.where(row_group == k, block[96:128], block[32 * k : 32 * k + 32]) for k in range(3)], axis=0
            )
            for h in range(2):
                spot = pl.ds(pl.multiple_of(win * (2 * i + h), 8), win)
                flat[spot, :] = block[WIN * h : WIN * h + win]
            return carry

        lax.fori_loop(0, 16, unpack, 0, unroll=16)
        for half in (slice(0, 16 * win), slice(16 * win, 32 * win)):
            mid[half, :] = fine_dot(flat[half, :], inv_ref[...])

        def finish(g, carry):
            def load(m):
                spot = pl.ds(pl.multiple_of(win * m + 8 * g, 8), 8)
                return mid[spot, 0:128], mid[spot, 128:256]

            values = inverse_outer(load, OUTER, turn_ref)

            def spot(t):
                return pl.ds(pl.multiple_of(win * t + 8 * g, 8), 8)

            if q == 0:
                for t in range(OUTER):
                    near[2, spot(t), :] = values[t]
                for d in (-2, -1, 1, 2):
                    moved = [pltpu.roll(v, (-d) % 128, 1) for v in values]
                    for t in range(OUTER):
                        if d < 0:
                            v = jnp.where(lane < -d, moved[t - 1], moved[t])
                        else:
                            v = jnp.where(lane < 128 - d, moved[t], moved[(t + 1) % OUTER])
                        near[2 + d, spot(t), :] = v
            else:
                moved = [pltpu.roll(v, 32, 1) for v in values]
                for t in range(OUTER):
                    even[spot(t), :] = jnp.where(lane < 32, moved[t - 1], moved[t])
                moved = [pltpu.roll(v, 96, 1) for v in values]
                for t in range(OUTER):
                    odd[spot(t), :] = jnp.where(lane < 96, moved[t], moved[(t + 1) % OUTER])
            return carry

        lax.fori_loop(0, win // 8, finish, 0, unroll=5 if q == 0 else 3)

    low_half = lane < 64

    def spot8(t):
        return pl.ds(pl.multiple_of(8 * t, 8), 8)

    def near_tile(t):
        cols = pl.ds(pl.multiple_of(128 * t, 128), 128)
        off_y = off_ref[0, :, cols]
        off_x = off_ref[1, :, cols]
        rel_y = 4.0 * off_y
        low_y = jnp.minimum(jnp.floor(rel_y), 1.0)
        left = off_x < 0.0
        frac_x = jnp.where(left, off_x + 1.0, off_x)
        bits = [low_y >= 0.0, (low_y == -1.0) | (low_y == 1.0)]
        taps = []
        for c in range(4):
            cells = []
            for j in range(4, 11):
                rows = pl.ds(NEAR_WIN * t + j, 8, stride=4)
                cells.append(jnp.where(left, near[c, rows, :], near[c + 1, rows, :]))
            cells = [jnp.where(bits[0], cells[k + 2], cells[k]) for k in range(5)]
            taps.append([jnp.where(bits[1], cells[k + 1], cells[k]) for k in range(4)])
        found = stencil(taps, spline_weights(frac_x), spline_weights(rel_y - low_y))
        pos_y = (7.0 + rel_y) - lens_ratio * found[0]
        start = (32 + lax.rem(lane, 64)).astype(jnp.float32)
        pos_x = (start + off_x) - lens_ratio * found[1]
        for i in range(5):
            first[i, spot8(t), :] = found[i]
        pos[0, spot8(t), :] = pos_x
        pos[1, spot8(t), :] = pos_y
        pos[2, spot8(t), :] = pltpu.roll(pos_x, 64, 1)
        pos[3, spot8(t), :] = pltpu.roll(pos_y, 64, 1)

    def far_tile(t):
        for side, (source, mask) in enumerate(((even, low_half), (odd, ~low_half))):
            block_x = jnp.where(mask, pos[0, spot8(t), :], pos[2, spot8(t), :])
            block_y = jnp.where(mask, pos[1, spot8(t), :], pos[3, spot8(t), :])
            low_x = jnp.floor(block_x)
            cell_x = jnp.clip(low_x, -8.0, 136.0).astype(jnp.int32) - jnp.where(low_half, 1, 0)
            cell_y = jnp.clip(jnp.floor(block_y), -8.0, 32.0).astype(jnp.int32) - 1
            weights = spline_weights(block_x - low_x)
            weights = [[jnp.where(low_half, w[2 * c], w[2 * c + 1]) for c in range(2)] for w in weights]
            spots = [cell_x, cell_x + 2]
            xw = kept(weights, spots, 128)
            bits = [(cell_y & b) != 0 for b in (8, 4, 2, 1)]
            taps = []
            for c in range(2):
                spot = jnp.clip(spots[c], 0, 127)
                cells = []
                for j in range(PATCH_ROWS):
                    cells.append(lane_gather(source[pl.ds(WIN * t + j, 8, stride=4), :], spot))
                cells = [jnp.where(bits[0], cells[(k + 8) % 16], cells[k]) for k in range(11)]
                cells = [jnp.where(bits[1], cells[k + 4], cells[k]) for k in range(7)]
                cells = [jnp.where(bits[2], cells[k + 2], cells[k]) for k in range(5)]
                taps.append([jnp.where(bits[3], cells[k + 1], cells[k]) for k in range(4)])
            for i, w in enumerate(xw):
                for r in range(4):
                    halves[side, 4 * i + r, spot8(t), :] = w[0] * taps[0][r] + w[1] * taps[1][r]

    def last_tile(t):
        cols = pl.ds(pl.multiple_of(128 * t, 128), 128)
        across = []
        for i in range(12):
            e, o = halves[0, i, spot8(t), :], halves[1, i, spot8(t), :]
            across.append(jnp.where(low_half, e, o) + pltpu.roll(jnp.where(low_half, o, e), 64, 1))
        pos_y = pos[1, spot8(t), :]
        low_y = jnp.floor(pos_y)
        cell_y = jnp.clip(low_y, -8.0, 32.0).astype(jnp.int32) - 1
        yw = kept(spline_weights(pos_y - low_y), [cell_y + c for c in range(4)], PATCH_ROWS)
        second = across_rows(across[0:4], across[4:8], across[8:12], yw)
        slope_y, slope_x, hess_yy, hess_xx, hess_xy = [first[i, spot8(t), :] for i in range(5)]
        other_yy, other_xx, other_xy = second[2], second[3], second[4]
        lensed_yy = 1.0 - lens_ratio * hess_yy
        lensed_xx = 1.0 - lens_ratio * hess_xx
        lensed_xy = -lens_ratio * hess_xy
        deflect_ref[0, :, cols] = slope_y + second[0]
        deflect_ref[1, :, cols] = slope_x + second[1]
        jacob_ref[0, :, cols] = 1.0 - hess_yy - (other_yy * lensed_yy + other_xy * lensed_xy)
        jacob_ref[1, :, cols] = -hess_xy - (other_yy * lensed_xy + other_xy * lensed_xx)
        jacob_ref[2, :, cols] = -hess_xy - (other_xy * lensed_yy + other_xx * lensed_xy)
        jacob_ref[3, :, cols] = 1.0 - hess_xx - (other_xy * lensed_xy + other_xx * lensed_xx)

    def several(step, count):
        def body(i, carry):
            for k in range(count):
                step(count * i + k)
            return carry

        return body

    def send(k):
        cols = pl.ds(pl.multiple_of(1024 * k, 1024), 1024)
        return [
            pltpu.make_async_copy(ref.at[:, :, cols], hbm.at[:, :, cols], sems.at[i, k])
            for i, (ref, hbm) in enumerate(((deflect_ref, deflect_hbm), (jacob_ref, jacob_hbm)))
        ]

    def body(i, carry):
        for k in range(FAR_STEP):
            last_tile(FAR_STEP * i - FAR_STEP + k)
            far_tile(FAR_STEP * i + k)
            near_tile(FAR_STEP * i + FAR_STEP + k)

        @pl.when(lax.rem(i, 2) == 0)
        def _():
            for copy in send(lax.div(i, 2) - 1):
                copy.start()

        return carry

    for k in range(FAR_STEP):
        near_tile(k)
    for k in range(FAR_STEP):
        far_tile(k)
        near_tile(FAR_STEP + k)
    lax.fori_loop(1, OUTER // FAR_STEP - 1, body, 0)
    for k in range(FAR_STEP):
        last_tile(OUTER - 2 * FAR_STEP + k)
        far_tile(OUTER - FAR_STEP + k)
    for k in range(FAR_STEP):
        last_tile(OUTER - FAR_STEP + k)
    for copy in send(3):
        copy.start()
    for k in range(4):
        for copy in send(k):
            copy.wait()


def vmem(shape):
    return pltpu.VMEM(shape, jnp.float32)


def call(kernel, name, args, outs, scratch, ins=None, out_space=pltpu.VMEM, grant=16 * 1024 * 1024):
    spaces = [pltpu.VMEM] * len(args) if ins is None else ins
    return pl.pallas_call(
        kernel,
        name=name,
        out_shape=outs,
        in_specs=[pl.BlockSpec(memory_space=space) for space in spaces],
        out_specs=jax.tree.map(lambda _: pl.BlockSpec(memory_space=out_space), outs),
        scratch_shapes=scratch,
        compiler_params=pltpu.CompilerParams(vmem_limit_bytes=grant),
    )(*args)


def shape(*dims):
    return jax.ShapeDtypeStruct(dims, jnp.float32)


def on_device(kappa, ray_offsets):
    tab = tables()
    spectra = call(
        rows_kernel,
        "rows",
        (kappa[0], tab["row_fwd"], tab["row_turn"]),
        shape(2048, 128),
        [
            vmem((2048, 128)),
            vmem((64, N)),
            pltpu.VMEM((256, 256), jnp.bfloat16),
            vmem((2, OUTER, 128)),
            vmem((2048, 256)),
            pltpu.SemaphoreType.DMA((14,)),
        ],
        ins=[pltpu.HBM] * 3,
        out_space=pltpu.HBM,
        grant=ROWS_GRANT,
    )
    columns = lax.all_to_all(spectra.reshape(SLABS, 32, 128), "slab", split_axis=0, concat_axis=0, tiled=True)
    strips = call(
        columns_kernel,
        "columns",
        (columns, tab["col_fwd"], tab["col_turn"], tab["wave2"], tab["col_inv"], tab["col_back"]),
        shape(2 * SLABS, 24, 128),
        [vmem((2, 512, 256)), vmem((2, 512, 128)), pltpu.VMEM((4, 512, 384), jnp.bfloat16)],
    )
    windows = lax.all_to_all(strips, ("plane", "slab"), split_axis=0, concat_axis=0, tiled=True)
    deflection, jacobian = call(
        rays_kernel,
        "rays",
        (windows, tab["row_inv"], tab["row_turn"], ray_offsets[:, 0, 0]),
        (shape(2, 8, N), shape(4, 8, N)),
        [
            vmem((2, 8, N)),
            vmem((4, 8, N)),
            vmem((OUTER * WIN, 128)),
            vmem((OUTER * WIN, 256)),
            vmem((5, OUTER * NEAR_WIN + 8, 128)),
            vmem((OUTER * WIN, 128)),
            vmem((OUTER * WIN, 128)),
            vmem((5, 8 * OUTER, 128)),
            vmem((4, 8 * OUTER, 128)),
            vmem((2, 12, 8 * OUTER, 128)),
            pltpu.SemaphoreType.DMA((2, 4)),
        ],
        grant=20 * 1024 * 1024,
        out_space=pltpu.HBM,
    )
    return deflection[:, None, None], jacobian[:, None, None]


def solution(mesh):
    placed = (P("plane", "slab", None), P(None, "slab", "plane", None, None))
    return jax.shard_map(
        on_device,
        mesh=mesh,
        in_specs=placed,
        out_specs=(P(None, "slab", "plane", None, None), P(None, "slab", "plane", None, None)),
        check_vma=False,
    )
```

```python
import functools
import math

import jax
import jax.numpy as jnp
import numpy as np
from jax import lax
from jax.experimental import pallas as pl
from jax.experimental.pallas import tpu as pltpu
from jax.sharding import PartitionSpec as P

N = 4096
OUTER = 32
SLABS = 64
PATCH_ROWS = 16
NEAR_WIN = 40
WIN = 48
ROWS_GRANT = 62 * 1024 * 1024
NEAR_STEP = 4
FAR_STEP = 4
LEAD = 5
lens_ratio = 0.5
screen_modes = 4.0


def angles(left, right, length):
    return (np.outer(left, right) % length) * (2.0 * np.pi / length)


def cas_pair(left, right, length):
    a = angles(left, right, length)
    return np.cos(a) + np.sin(a), np.cos(a) - np.sin(a)


def f32(table):
    return np.asarray(table, np.float32)


def parts(table, count):
    out = []
    for _ in range(count):
        out.append(np.asarray(table, jnp.bfloat16))
        table = table - np.asarray(out[-1], np.float64)
    return out


@functools.cache
def tables():
    out = {}
    lane = np.arange(128)
    plus, minus = cas_pair(lane, lane, 128)
    both = np.concatenate([plus, minus], axis=0)
    out["row_fwd"] = np.concatenate(parts(both, 2), axis=1)
    turn = angles(np.arange(OUTER), lane, N)
    out["row_turn"] = f32(np.stack([np.cos(turn), np.sin(turn)]))
    out["row_inv"] = np.stack(parts(0.5 * np.concatenate([plus, -minus], axis=1), 3))
    sixty = np.arange(64)
    plus, minus = cas_pair(sixty, sixty, 64)
    two = np.eye(2)
    both = np.concatenate([np.kron(two, plus), np.kron(two, minus)], axis=0)
    out["col_fwd"] = np.concatenate(parts(both, 2), axis=1)
    turn = angles(sixty, np.concatenate([sixty, sixty]), N)
    out["col_turn"] = f32(np.stack([np.cos(turn), np.sin(turn)]))
    inv, turns = [], []
    for p in range(2):
        rows = 32 * p - LEAD + np.arange(WIN)
        plus, minus = cas_pair(sixty, rows, 64)
        table = 0.5 * np.stack([np.kron(two, plus), -np.kron(two, minus)], axis=1)
        turn = angles(sixty, np.concatenate([rows, rows]), N)
        for k in range(3):
            own = slice(32 * k, 32 * k + 32)
            inv.append(np.concatenate([table, table[:, :, own]], axis=2).reshape(128, 256))
            full = np.concatenate([turn, turn[:, own]], axis=1)
            turns.append(np.stack([np.cos(full), np.sin(full)]))
    out["col_inv"] = np.stack([np.stack(parts(table, 3)) for table in inv]).reshape(2, 3, 3, 128, 256)
    out["col_back"] = f32(np.stack(turns).reshape(2, 3, 2, 64, 128))
    ids = np.arange(64)[:, None] + 64 * np.concatenate([sixty, sixty])[None, :]
    wave = 2.0 * np.pi / N * np.minimum(ids, N - ids)
    out["wave2"] = f32(wave**2)
    return out


def cmul(re, im, c, s):
    if abs(s) < 1e-12 and abs(c - 1.0) < 1e-12:
        return re, im
    if abs(c) < 1e-12 and abs(s - 1.0) < 1e-12:
        return (None if im is None else -im), re
    if im is None:
        return re * c, re * s
    if re is None:
        return im * (-s), im * c
    if abs(c - s) < 1e-12:
        return (re - im) * c, (re + im) * c
    if abs(c + s) < 1e-12:
        return (re + im) * c, (im - re) * c
    return re * c - im * s, re * s + im * c


def add(a, b):
    return b if a is None else a if b is None else a + b


def sub(a, b):
    return a if b is None else -b if a is None else a - b


def neg(a):
    return None if a is None else -a


def real_to_half(xs):
    n = len(xs)
    if n == 2:
        return [(xs[0] + xs[1], None), (xs[0] - xs[1], None)]
    even, odd = real_to_half(xs[0::2]), real_to_half(xs[1::2])
    half = n // 2
    out = [None] * (half + 1)
    for k in range(half // 2 + 1):
        c, s = math.cos(2 * math.pi * k / n), math.sin(2 * math.pi * k / n)
        tr, ti = cmul(*odd[k], c, s)
        er, ei = even[k]
        out[k] = (add(er, tr), add(ei, ti))
        if half - k != k:
            out[half - k] = (sub(er, tr), sub(ti, ei))
    return out


def half_to_real(xs):
    half = len(xs) - 1
    n = 2 * half
    if n == 2:
        return [xs[0][0] + xs[1][0], xs[0][0] - xs[1][0]]
    even, odd = [], []
    for k in range(half // 2 + 1):
        ar, ai = xs[k]
        br, bi = xs[half - k]
        if k == half - k:
            even.append((ar + ar, None))
            odd.append((-(ai + ai), None))
            continue
        even.append((add(ar, br), sub(ai, bi)))
        c, s = math.cos(2 * math.pi * k / n), math.sin(2 * math.pi * k / n)
        odd.append(cmul(sub(ar, br), add(ai, bi), c, s))
    evens, odds = half_to_real(even), half_to_real(odd)
    return [v for pair in zip(evens, odds) for v in pair]


def row8(ref, *index):
    return jnp.broadcast_to(ref[index], (8, 128))


def turned(re, im, c, s):
    if im is None:
        return re * c, re * s
    return re * c - im * s, re * s + im * c


def forward_outer(xs, turn_ref, store):
    n = len(xs)
    half = real_to_half(xs)
    for m in range(n):
        re, im = half[m] if m <= n // 2 else (half[n - m][0], neg(half[n - m][1]))
        store(m, *turned(re, im, row8(turn_ref, 0, slice(m, m + 1)), row8(turn_ref, 1, slice(m, m + 1))))


def inverse_outer(load, n, turn_ref, *lead):
    def value(m):
        re, im = load(m)
        return turned(re, im, row8(turn_ref, *lead, 0, slice(m, m + 1)), row8(turn_ref, *lead, 1, slice(m, m + 1)))

    spectrum = []
    for m in range(n // 2 + 1):
        re, im = value(m)
        if m in (0, n // 2):
            spectrum.append((re + re, None))
        else:
            ro, io = value(n - m)
            spectrum.append((re + ro, im - io))
    return half_to_real(spectrum)


def split(x, count):
    out = []
    for i in range(count):
        out.append(x.astype(jnp.bfloat16))
        if i + 1 < count:
            x = x - out[-1].astype(jnp.float32)
    return out


def left_of(pieces):
    a, b, c = (pieces[:, 128 * i : 128 * i + 128] for i in range(3))
    return [a, b, a, b, a, c]


def right_of(w):
    return [w[0], w[0], w[1], w[1], w[2], w[0]]


def fine_dot(x, w):
    left = jnp.concatenate(left_of(jnp.concatenate(split(x, 3), axis=1)), axis=1)
    return jnp.dot(left, jnp.concatenate(right_of(w), axis=0), preferred_element_type=jnp.float32)


def coarse_dot(x, w):
    left = jnp.concatenate(split(x, 2), axis=1)
    both = jnp.dot(left, jnp.concatenate([w, w], axis=0), preferred_element_type=jnp.float32)
    return both[:, :128] + both[:, 128:]


def rows_kernel(kappa_hbm, weight_hbm, turn_hbm, out_hbm, out_ref, kappa_ref, weight_ref, turn_ref, mid, sems):
    def fetch(g):
        rows = pl.ds(8 * g, 8)
        return pltpu.make_async_copy(kappa_hbm.at[rows, :], kappa_ref.at[rows, :], sems.at[g])

    def send(i):
        rows = pl.ds(512 * i, 512)
        return pltpu.make_async_copy(out_ref.at[rows, :], out_hbm.at[rows, :], sems.at[10 + i])

    turn_copy = pltpu.make_async_copy(turn_hbm, turn_ref, sems.at[8])
    weight_copy = pltpu.make_async_copy(weight_hbm, weight_ref, sems.at[9])
    turn_copy.start()
    for g in range(8):
        fetch(g).start()
    weight_copy.start()
    turn_copy.wait()
    for g in range(8):
        fetch(g).wait()
        xs = [kappa_ref[8 * g : 8 * g + 8, 128 * j : 128 * j + 128] for j in range(OUTER)]

        def store(m, re, im):
            mid[64 * m + 8 * g : 64 * m + 8 * g + 8, 0:128] = re
            mid[64 * m + 8 * g : 64 * m + 8 * g + 8, 128:256] = im

        forward_outer(xs, turn_ref, store)
    weight_copy.wait()
    for i in range(4):
        found = coarse_dot(mid[512 * i : 512 * i + 512, :], weight_ref[...])
        for k in range(4):
            out_ref[512 * i + 128 * k : 512 * i + 128 * k + 128, :] = jnp.transpose(found[128 * k : 128 * k + 128])
        send(i).start()
    for i in range(4):
        send(i).wait()


def columns_kernel(in_ref, fwd_ref, turn_ref, wave_ref, inv_ref, back_ref, out_ref, mids, specs, pieces):
    owner = lax.axis_index("slab")
    base = 2 * lax.div(owner, 4) + 1024 * lax.rem(owner, 4)
    lane = lax.broadcasted_iota(jnp.int32, (8, 128), 1)
    sub8 = lax.broadcasted_iota(jnp.int32, (8, 128), 0)
    screen = (2.0 * math.pi * screen_modes / N) ** 2

    def forward(g, mid, spec):
        rows = pl.ds(pl.multiple_of(8 * g, 8), 8)
        xs = [in_ref[s, rows, :] for s in range(SLABS)]

        def store(m, re, im):
            mid[8 * m : 8 * m + 8, 0:128] = re
            mid[8 * m : 8 * m + 8, 128:256] = im

        forward_outer(xs, turn_ref, store)
        spec[...] = coarse_dot(mid[...], fwd_ref[...])
        ids = base + jnp.where(lane >= 64, 1, 0) + 32 * (8 * g + sub8)
        wave = (2.0 * math.pi / N) * jnp.minimum(ids, N - ids).astype(jnp.float32)
        mine = wave * wave + screen
        for m in range(SLABS):
            factor = -2.0 / ((mine + row8(wave_ref, slice(m, m + 1))) * float(N * N))
            if m == 0:
                factor = jnp.where((ids == 0) & (lane == 0), 0.0, factor)
            spec[8 * m : 8 * m + 8, :] = spec[8 * m : 8 * m + 8, :] * factor
        for i, piece in enumerate(split(spec[...], 3)):
            pieces[g, :, 128 * i : 128 * i + 128] = piece

    def forward_pair(i, carry):
        forward(2 * i, mids.at[0], specs.at[0])
        forward(2 * i + 1, mids.at[1], specs.at[1])
        return carry

    lax.fori_loop(0, 2, forward_pair, 0, unroll=2)

    def backward(k, carry):
        slot = lax.rem(lax.broadcasted_iota(jnp.int32, (128, 256), 1), 128) // 32
        given = jnp.where(slot == k, 1.0, 0.0)
        taken, given = (1.0 - given).astype(jnp.bfloat16), given.astype(jnp.bfloat16)
        for p in range(2):
            mid = mids.at[p]
            left = left_of(pieces[k]) + left_of(pieces[3])
            right = right_of([inv_ref[p, k, i] * taken for i in range(3)])
            right += right_of([inv_ref[p, k, i] * given for i in range(3)])
            mid[...] = jnp.dot(
                jnp.concatenate(left, axis=1), jnp.concatenate(right, axis=0), preferred_element_type=jnp.float32
            )
            values = inverse_outer(
                lambda m: (mid[8 * m : 8 * m + 8, 0:128], mid[8 * m : 8 * m + 8, 128:256]), SLABS, back_ref, p, k
            )
            rows = pl.ds(pl.multiple_of(8 * k, 8), 8)
            for s in range(SLABS):
                out_ref[p * SLABS + s, rows, :] = values[s]
        return carry

    lax.fori_loop(0, 3, backward, 0, unroll=3)


def spline_weights(f):
    e = 1.0 - f
    f2, e2 = f * f, e * e
    f3, e3 = f2 * f, e2 * e
    sixth, third = 1.0 / 6.0, 2.0 / 3.0
    value = [e3 * sixth, third - f2 + 0.5 * f3, third - e2 + 0.5 * e3, f3 * sixth]
    slope = [-0.5 * e2, 1.5 * f2 - 2.0 * f, 2.0 * e - 1.5 * e2, 0.5 * f2]
    curve = [e, 3.0 * f - 2.0, 1.0 - 3.0 * f, f]
    return value, slope, curve


def dot4(ws, vs):
    return (ws[0] * vs[0] + ws[1] * vs[1]) + (ws[2] * vs[2] + ws[3] * vs[3])


def stencil(taps, xw, yw):
    rows = list(zip(*taps))
    flat = [dot4(xw[0], row) for row in rows]
    slope = [dot4(xw[1], row) for row in rows]
    curve = [dot4(xw[2], row) for row in rows]
    return across_rows(flat, slope, curve, yw)


def across_rows(flat, slope, curve, yw):
    return dot4(yw[1], flat), dot4(yw[0], slope), dot4(yw[2], flat), dot4(yw[0], curve), dot4(yw[1], slope)


def kept(weights, cells, count):
    inside = [(cell >= 0) & (cell < count) for cell in cells]
    return [[jnp.where(inside[c], w[c], 0.0) for c in range(len(cells))] for w in weights]


def lane_gather(values, spots):
    dims = lax.GatherDimensionNumbers(
        offset_dims=(), collapsed_slice_dims=(1,), start_index_map=(1,),
        operand_batching_dims=(0,), start_indices_batching_dims=(0,),
    )
    return lax.gather(
        values, spots[..., None], dims, (1, 1), mode=lax.GatherScatterMode.PROMISE_IN_BOUNDS
    )


def rays_kernel(
    in_ref, inv_ref, turn_ref, off_ref, deflect_hbm, jacob_hbm, deflect_ref, jacob_ref, flat, mid, near, even, odd, first, pos, halves, sems
):
    lane = lax.broadcasted_iota(jnp.int32, (8, 128), 1)

    row_group = lax.rem(lax.broadcasted_iota(jnp.int32, (32, 128), 1), 32) // 8

    for q, win in enumerate((NEAR_WIN, WIN)):
        def unpack(i, carry):
            rows = []
            for d in range(4):
                got = [in_ref[q * SLABS + 4 * i + d, 8 * k : 8 * k + 8, :] for k in range(3)]
                rows += got
                rows.append(jnp.where(lane < 32, got[0], jnp.where(lane < 64, got[1], got[2])))
            block = jnp.transpose(jnp.concatenate(rows, axis=0))
            block = jnp.concatenate(
                [jnp.where(row_group == k, block[96:128], block[32 * k : 32 * k + 32]) for k in range(3)], axis=0
            )
            for h in range(2):
                spot = pl.ds(pl.multiple_of(win * (2 * i + h), 8), win)
                flat[spot, :] = block[WIN * h : WIN * h + win]
            return carry

        lax.fori_loop(0, 16, unpack, 0, unroll=16)
        for half in (slice(0, 16 * win), slice(16 * win, 32 * win)):
            mid[half, :] = fine_dot(flat[half, :], inv_ref[...])

        def finish(g, carry):
            def load(m):
                spot = pl.ds(pl.multiple_of(win * m + 8 * g, 8), 8)
                return mid[spot, 0:128], mid[spot, 128:256]

            values = inverse_outer(load, OUTER, turn_ref)

            def spot(t):
                return pl.ds(pl.multiple_of(win * t + 8 * g, 8), 8)

            if q == 0:
                for t in range(OUTER):
                    near[2, spot(t), :] = values[t]
                for d in (-2, -1, 1, 2):
                    moved = [pltpu.roll(v, (-d) % 128, 1) for v in values]
                    for t in range(OUTER):
                        if d < 0:
                            v = jnp.where(lane < -d, moved[t - 1], moved[t])
                        else:
                            v = jnp.where(lane < 128 - d, moved[t], moved[(t + 1) % OUTER])
                        near[2 + d, spot(t), :] = v
            else:
                moved = [pltpu.roll(v, 32, 1) for v in values]
                for t in range(OUTER):
                    even[spot(t), :] = jnp.where(lane < 32, moved[t - 1], moved[t])
                moved = [pltpu.roll(v, 96, 1) for v in values]
                for t in range(OUTER):
                    odd[spot(t), :] = jnp.where(lane < 96, moved[t], moved[(t + 1) % OUTER])
            return carry

        lax.fori_loop(0, win // 8, finish, 0, unroll=win // 8)

    low_half = lane < 64

    def spot8(t):
        return pl.ds(pl.multiple_of(8 * t, 8), 8)

    def near_tile(t):
        cols = pl.ds(pl.multiple_of(128 * t, 128), 128)
        off_y = off_ref[0, :, cols]
        off_x = off_ref[1, :, cols]
        rel_y = 4.0 * off_y
        low_y = jnp.minimum(jnp.floor(rel_y), 1.0)
        left = off_x < 0.0
        frac_x = jnp.where(left, off_x + 1.0, off_x)
        bits = [low_y >= 0.0, (low_y == -1.0) | (low_y == 1.0)]
        taps = []
        for c in range(4):
            cells = []
            for j in range(4, 11):
                rows = pl.ds(NEAR_WIN * t + j, 8, stride=4)
                cells.append(jnp.where(left, near[c, rows, :], near[c + 1, rows, :]))
            cells = [jnp.where(bits[0], cells[k + 2], cells[k]) for k in range(5)]
            taps.append([jnp.where(bits[1], cells[k + 1], cells[k]) for k in range(4)])
        found = stencil(taps, spline_weights(frac_x), spline_weights(rel_y - low_y))
        pos_y = (7.0 + rel_y) - lens_ratio * found[0]
        start = (32 + lax.rem(lane, 64)).astype(jnp.float32)
        pos_x = (start + off_x) - lens_ratio * found[1]
        for i in range(5):
            first[i, spot8(t), :] = found[i]
        pos[0, spot8(t), :] = pos_x
        pos[1, spot8(t), :] = pos_y
        pos[2, spot8(t), :] = pltpu.roll(pos_x, 64, 1)
        pos[3, spot8(t), :] = pltpu.roll(pos_y, 64, 1)

    def far_tile(t):
        for side, (source, mask) in enumerate(((even, low_half), (odd, ~low_half))):
            block_x = jnp.where(mask, pos[0, spot8(t), :], pos[2, spot8(t), :])
            block_y = jnp.where(mask, pos[1, spot8(t), :], pos[3, spot8(t), :])
            low_x = jnp.floor(block_x)
            cell_x = jnp.clip(low_x, -8.0, 136.0).astype(jnp.int32) - jnp.where(low_half, 1, 0)
            cell_y = jnp.clip(jnp.floor(block_y), -8.0, 32.0).astype(jnp.int32) - 1
            weights = spline_weights(block_x - low_x)
            weights = [[jnp.where(low_half, w[2 * c], w[2 * c + 1]) for c in range(2)] for w in weights]
            spots = [cell_x, cell_x + 2]
            xw = kept(weights, spots, 128)
            bits = [(cell_y & b) != 0 for b in (8, 4, 2, 1)]
            taps = []
            for c in range(2):
                spot = jnp.clip(spots[c], 0, 127)
                cells = []
                for j in range(PATCH_ROWS):
                    cells.append(lane_gather(source[pl.ds(WIN * t + j, 8, stride=4), :], spot))
                cells = [jnp.where(bits[0], cells[(k + 8) % 16], cells[k]) for k in range(11)]
                cells = [jnp.where(bits[1], cells[k + 4], cells[k]) for k in range(7)]
                cells = [jnp.where(bits[2], cells[k + 2], cells[k]) for k in range(5)]
                taps.append([jnp.where(bits[3], cells[k + 1], cells[k]) for k in range(4)])
            for i, w in enumerate(xw):
                for r in range(4):
                    halves[side, 4 * i + r, spot8(t), :] = w[0] * taps[0][r] + w[1] * taps[1][r]

    def last_tile(t):
        cols = pl.ds(pl.multiple_of(128 * t, 128), 128)
        across = []
        for i in range(12):
            e, o = halves[0, i, spot8(t), :], halves[1, i, spot8(t), :]
            across.append(jnp.where(low_half, e, o) + pltpu.roll(jnp.where(low_half, o, e), 64, 1))
        pos_y = pos[1, spot8(t), :]
        low_y = jnp.floor(pos_y)
        cell_y = jnp.clip(low_y, -8.0, 32.0).astype(jnp.int32) - 1
        yw = kept(spline_weights(pos_y - low_y), [cell_y + c for c in range(4)], PATCH_ROWS)
        second = across_rows(across[0:4], across[4:8], across[8:12], yw)
        slope_y, slope_x, hess_yy, hess_xx, hess_xy = [first[i, spot8(t), :] for i in range(5)]
        other_yy, other_xx, other_xy = second[2], second[3], second[4]
        lensed_yy = 1.0 - lens_ratio * hess_yy
        lensed_xx = 1.0 - lens_ratio * hess_xx
        lensed_xy = -lens_ratio * hess_xy
        deflect_ref[0, :, cols] = slope_y + second[0]
        deflect_ref[1, :, cols] = slope_x + second[1]
        jacob_ref[0, :, cols] = 1.0 - hess_yy - (other_yy * lensed_yy + other_xy * lensed_xy)
        jacob_ref[1, :, cols] = -hess_xy - (other_yy * lensed_xy + other_xy * lensed_xx)
        jacob_ref[2, :, cols] = -hess_xy - (other_xy * lensed_yy + other_xx * lensed_xy)
        jacob_ref[3, :, cols] = 1.0 - hess_xx - (other_xy * lensed_xy + other_xx * lensed_xx)

    def several(step, count):
        def body(i, carry):
            for k in range(count):
                step(count * i + k)
            return carry

        return body

    def send(k):
        cols = pl.ds(pl.multiple_of(1024 * k, 1024), 1024)
        return [
            pltpu.make_async_copy(ref.at[:, :, cols], hbm.at[:, :, cols], sems.at[i, k])
            for i, (ref, hbm) in enumerate(((deflect_ref, deflect_hbm), (jacob_ref, jacob_hbm)))
        ]

    def body(i, carry):
        for k in range(FAR_STEP):
            last_tile(FAR_STEP * i - FAR_STEP + k)
            far_tile(FAR_STEP * i + k)
            near_tile(FAR_STEP * i + FAR_STEP + k)

        @pl.when(lax.rem(i, 2) == 0)
        def _():
            for copy in send(lax.div(i, 2) - 1):
                copy.start()

        return carry

    for k in range(FAR_STEP):
        near_tile(k)
    for k in range(FAR_STEP):
        far_tile(k)
        near_tile(FAR_STEP + k)
    lax.fori_loop(1, OUTER // FAR_STEP - 1, body, 0)
    for k in range(FAR_STEP):
        last_tile(OUTER - 2 * FAR_STEP + k)
        far_tile(OUTER - FAR_STEP + k)
    for k in range(FAR_STEP):
        last_tile(OUTER - FAR_STEP + k)
    for copy in send(3):
        copy.start()
    for k in range(4):
        for copy in send(k):
            copy.wait()


def vmem(shape):
    return pltpu.VMEM(shape, jnp.float32)


def call(kernel, name, args, outs, scratch, ins=None, out_space=pltpu.VMEM, grant=16 * 1024 * 1024):
    spaces = [pltpu.VMEM] * len(args) if ins is None else ins
    return pl.pallas_call(
        kernel,
        name=name,
        out_shape=outs,
        in_specs=[pl.BlockSpec(memory_space=space) for space in spaces],
        out_specs=jax.tree.map(lambda _: pl.BlockSpec(memory_space=out_space), outs),
        scratch_shapes=scratch,
        compiler_params=pltpu.CompilerParams(vmem_limit_bytes=grant),
    )(*args)


def shape(*dims):
    return jax.ShapeDtypeStruct(dims, jnp.float32)


def on_device(kappa, ray_offsets):
    tab = tables()
    spectra = call(
        rows_kernel,
        "rows",
        (kappa[0], tab["row_fwd"], tab["row_turn"]),
        shape(2048, 128),
        [
            vmem((2048, 128)),
            vmem((64, N)),
            pltpu.VMEM((256, 256), jnp.bfloat16),
            vmem((2, OUTER, 128)),
            vmem((2048, 256)),
            pltpu.SemaphoreType.DMA((14,)),
        ],
        ins=[pltpu.HBM] * 3,
        out_space=pltpu.HBM,
        grant=ROWS_GRANT,
    )
    columns = lax.all_to_all(spectra.reshape(SLABS, 32, 128), "slab", split_axis=0, concat_axis=0, tiled=True)
    strips = call(
        columns_kernel,
        "columns",
        (columns, tab["col_fwd"], tab["col_turn"], tab["wave2"], tab["col_inv"], tab["col_back"]),
        shape(2 * SLABS, 24, 128),
        [vmem((2, 512, 256)), vmem((2, 512, 128)), pltpu.VMEM((4, 512, 384), jnp.bfloat16)],
    )
    windows = lax.all_to_all(strips, ("plane", "slab"), split_axis=0, concat_axis=0, tiled=True)
    deflection, jacobian = call(
        rays_kernel,
        "rays",
        (windows, tab["row_inv"], tab["row_turn"], ray_offsets[:, 0, 0]),
        (shape(2, 8, N), shape(4, 8, N)),
        [
            vmem((2, 8, N)),
            vmem((4, 8, N)),
            vmem((OUTER * WIN, 128)),
            vmem((OUTER * WIN, 256)),
            vmem((5, OUTER * NEAR_WIN + 8, 128)),
            vmem((OUTER * WIN, 128)),
            vmem((OUTER * WIN, 128)),
            vmem((5, 8 * OUTER, 128)),
            vmem((4, 8 * OUTER, 128)),
            vmem((2, 12, 8 * OUTER, 128)),
            pltpu.SemaphoreType.DMA((2, 4)),
        ],
        grant=20 * 1024 * 1024,
        out_space=pltpu.HBM,
    )
    return deflection[:, None, None], jacobian[:, None, None]


def solution(mesh):
    placed = (P("plane", "slab", None), P(None, "slab", "plane", None, None))
    return jax.shard_map(
        on_device,
        mesh=mesh,
        in_specs=placed,
        out_specs=(P(None, "slab", "plane", None, None), P(None, "slab", "plane", None, None)),
        check_vma=False,
    )
```
